32 devices in a mesh: lon: 16 (over z, y, x), lat: 2 (over core).
Axes of the slice: x: 2, y: 2, z: 4, core: 2. Of those that a mesh axis runs over, the one named last changes fastest.
Arguments:
- sketch: float32 [64, 256, 512], P(None, 'lon', 'lat'), may hold values from -6 to 6
- probe_bits: int32 [2, 256, 512], P(None, 'lon', 'lat'), may hold values from 0 to 65535
- ocean: int32 [256, 512], P('lon', 'lat'), may hold values 0 or 1
- east_cond: float32 [256, 512], P('lon', 'lat'), may hold values from 0.2 to 2
- north_cond: float32 [256, 512], P('lon', 'lat'), may hold values from 0.1 to 1
- kappa_sq: float32 [256, 512], P('lon', 'lat'), may hold values from 0.05 to 0.5
- inv_area: float32 [256, 512], P('lon', 'lat'), may hold values from 0.05 to 0.2
Outputs:
- image_out: float32 [64, 256, 512], P(None, 'lon', 'lat')
- gram_out: float32 [96, 96], replicated
The draws below stay inside these ranges and needn't reach their ends.
Inputs may be any that keep to these rules, and one draw needn't show every extreme that they name: `probe_bits`: each word holds 16 independent sign bits, bit b of word w giving probe column 16 w + b.
All inputs are finite; a program needn't handle non-finite values. No bound on the sum of `ocean` on one device may be relied on, other than what follows from the above.
Results may differ from the reference program's by a relative error of at most 0.00015.
Values sent between devices are 32-bit elements; how exact they have to be, the bound alone decides.
No kernel may reach another device: no remote copies, remote signals or barrier semaphores. Data moves between devices by JAX's collectives and lax.ppermute only.
A program may use at most 64 MiB of HBM per device.

```python
import math
import jax
import jax.numpy as jnp
from jax import lax

SKETCH = 64
WORDS = 2
NLON = 256
NLAT = 512


def place_ends(drawn, rng, least, high):
    longest = drawn.shape.index(max(drawn.shape))
    spots = []
    for shift in (0, 1):
        where = [jax.random.randint(jax.random.fold_in(rng, axis), (), 0, length) for axis, length in enumerate(drawn.shape)]
        where[longest] = (where[longest] + shift) % drawn.shape[longest]
        spots.append(tuple(where))
    return drawn.at[spots[0]].set(least).at[spots[1]].set(high)


def steps_of(own_key, extent, split, low, top_value):
    loudness = 1.0
    for position, shards_of in split:
        draws = jax.random.uniform(jax.random.fold_in(jax.random.fold_in(own_key, 6), position), (shards_of,), jnp.float32, low / len(split), top_value / len(split))
        loudness = loudness * jnp.repeat(jnp.exp(draws), extent[position] // shards_of).reshape((-1,) + (1,) * (len(extent) - 1 - position))
    return loudness


def gaussian(stream_key, shape, spread, limit, pieces=(), kind=jnp.bfloat16):
    factor_of = steps_of(stream_key, shape, pieces, -0.22, 0.18) if pieces else 1.0
    result = jax.random.normal(stream_key, shape, jnp.float32) * spread * factor_of
    return jnp.minimum(jnp.maximum(result, -limit), limit).astype(kind)


def setup_inputs(seed: int = 0) -> dict:
    keys = jax.random.split(jax.random.key(seed), 8)
    return {
        "sketch": gaussian(keys[0], (SKETCH, NLON, NLAT), 1.0, 6.0, ((1, 16), (2, 2)), jnp.float32),
        "probe_bits": place_ends(jax.random.randint(keys[1], (WORDS, NLON, NLAT), 0, 65536), jax.random.fold_in(keys[1], 1), 0, 65535).astype(jnp.int32),
        "ocean": place_ends((jax.random.randint(keys[2], (NLON, NLAT), 0, 4) < 3).astype(jnp.int32), jax.random.fold_in(keys[2], 1), 0, 1),
        "east_cond": jnp.clip(jnp.exp(math.log(2.0) - 2.3025851 * jax.random.uniform(keys[3], (NLON, NLAT), jnp.float32) ** steps_of(keys[3], (NLON, NLAT), ((0, 16), (1, 2)), -0.2, 0.2)), 0.2, 2.0),
        "north_cond": jnp.clip(jnp.exp(math.log(1.0) - 2.3025851 * jax.random.uniform(keys[4], (NLON, NLAT), jnp.float32) ** steps_of(keys[4], (NLON, NLAT), ((0, 16), (1, 2)), -0.2, 0.2)), 0.1, 1.0),
        "kappa_sq": jnp.clip(jnp.exp(math.log(0.5) - 2.3025851 * jax.random.uniform(keys[5], (NLON, NLAT), jnp.float32) ** steps_of(keys[5], (NLON, NLAT), ((0, 16), (1, 2)), -0.2, 0.2)), 0.05, 0.5),
        "inv_area": jnp.clip(jnp.exp(math.log(0.2) - 1.3862944 * jax.random.uniform(keys[6], (NLON, NLAT), jnp.float32) ** steps_of(keys[6], (NLON, NLAT), ((0, 16), (1, 2)), -0.2, 0.2)), 0.05, 0.2),
    }


def sign_columns(probe_bits):
    shifts = jnp.arange(16, dtype=jnp.int32)
    picked = jnp.right_shift(probe_bits[:, None], shifts[None, :, None, None])
    flipped = jnp.bitwise_and(picked, 1)
    return (1 - 2 * flipped).astype(jnp.float32).reshape((-1,) + probe_bits.shape[1:])


def reference(sketch, probe_bits, ocean, east_cond, north_cond, kappa_sq, inv_area):
    sea_mask = ocean.astype(jnp.float32)
    column_zero = jnp.zeros((sea_mask.shape[0], 1), jnp.float32)
    east_weight = east_cond * sea_mask * jnp.roll(sea_mask, -1, axis=0)
    north_mask = jnp.concatenate([sea_mask[:, 1:], column_zero], axis=1)
    north_weight = north_cond * sea_mask * north_mask
    west_weight = jnp.roll(east_weight, 1, axis=0)
    south_weight = jnp.concatenate([column_zero, north_weight[:, :-1]], axis=1)
    center_term = kappa_sq + east_weight + west_weight + north_weight + south_weight

    def operate(field_in):
        edge_zero = jnp.zeros(field_in.shape[:2] + (1,), jnp.float32)
        east_val = jnp.roll(field_in, -1, axis=1)
        west_val = jnp.roll(field_in, 1, axis=1)
        north_val = jnp.concatenate([field_in[:, :, 1:], edge_zero], axis=2)
        south_val = jnp.concatenate([edge_zero, field_in[:, :, :-1]], axis=2)
        return sea_mask * (center_term * field_in - east_weight * east_val - west_weight * west_val
                           - north_weight * north_val - south_weight * south_val)

    columns = jnp.concatenate([sketch, sign_columns(probe_bits)], axis=0) * sea_mask
    width_all = columns.shape[0]
    blocks = columns.reshape(width_all // 16, 16, NLON, NLAT)
    flat_all = columns.reshape(width_all, -1)

    def one_block(block):
        second = operate(inv_area * operate(block))
        part_gram = jnp.dot(second.reshape(16, -1), flat_all.T, precision=lax.Precision.HIGHEST)
        return second, part_gram

    seconds, gram_rows = lax.map(one_block, blocks)
    image_out = seconds.reshape(width_all, NLON, NLAT)[:SKETCH]
    gram_out = gram_rows.reshape(width_all, width_all) / (NLON * NLAT)
    return image_out, gram_out
```

```python
import jax
import jax.numpy as jnp
from jax import lax
from jax.sharding import PartitionSpec as P


def padded_2(cells, sides, width, closed):
    for axis, dim in sides:
        count = lax.axis_size(axis)
        ends = count if closed else count - 1
        head = lax.slice_in_dim(cells, 0, width, axis=dim)
        tail = lax.slice_in_dim(cells, cells.shape[dim] - width, cells.shape[dim], axis=dim)
        cells = jnp.concatenate(
            [
                lax.ppermute(tail, axis, [(i, (i + 1) % count) for i in range(ends)]),
                cells,
                lax.ppermute(head, axis, [((i + 1) % count, i) for i in range(ends)]),
            ],
            axis=dim,
        )
    return cells


def sign_columns(probe_bits):
    shifts = jnp.arange(16, dtype=jnp.int32)
    picked = jnp.right_shift(probe_bits[:, None], shifts[None, :, None, None])
    flipped = jnp.bitwise_and(picked, 1)
    return (1 - 2 * flipped).astype(jnp.float32).reshape((-1,) + probe_bits.shape[1:])


def operate(padded, weights):
    middle = padded[:, 1:-1, 1:-1]
    return weights[0] * (
        weights[1] * middle
        - weights[2] * padded[:, 2:, 1:-1]
        - weights[3] * padded[:, :-2, 1:-1]
        - weights[4] * padded[:, 1:-1, 2:]
        - weights[5] * padded[:, 1:-1, :-2]
    )


def extend(field_in, thickness):
    wider = padded_2(field_in, (("lon", 1),), thickness, True)
    return padded_2(wider, (("lat", 2),), thickness, False)


def pair_gram(left, right):
    left_flat = left.reshape(left.shape[0], -1)
    right_flat = right.reshape(right.shape[0], -1)
    return jnp.einsum("ac,bc->ab", left_flat, right_flat, precision=lax.Precision.HIGHEST)


def mesh_sum(part):
    lons, lats = lax.axis_size("lon"), lax.axis_size("lat")
    if lons & (lons - 1) or lats & (lats - 1):
        return lax.psum(part, ("lon", "lat"))
    step = 1
    while step < lats:
        part = part + lax.ppermute(part, "lat", [(i, i ^ step) for i in range(lats)])
        step *= 2
    step = 1
    while step < lons:
        pairs = [
            (i * lats + j, (i ^ step) * lats + (lats - 1 - j)) for i in range(lons) for j in range(lats)
        ]
        part = part + lax.ppermute(part, ("lon", "lat"), pairs)
        step *= 2
    return part


def local(sketch, probe_bits, ocean, east_cond, north_cond, kappa_sq, inv_area):
    lon_count, lat_count = ocean.shape
    sea_mask = ocean.astype(jnp.float32)
    stacked = jnp.stack([sea_mask, east_cond, north_cond, kappa_sq, inv_area])
    widened = padded_2(stacked, (("lon", 1),), 2, True)
    widened = padded_2(widened, (("lat", 2),), 2, False)
    sea_wide = widened[0]
    east_wide = widened[1]
    north_wide = widened[2]
    kappa_wide = widened[3]
    area_wide = widened[4]
    east_edges = east_wide[:-1] * sea_wide[:-1] * sea_wide[1:]
    north_edges = north_wide[:, :-1] * sea_wide[:, :-1] * sea_wide[:, 1:]
    offset = 2 - 0
    span_lon = lon_count + 2 * 0
    span_lat = lat_count + 2 * 0

    def window(array, shift_lon, shift_lat):
        return array[
            offset + shift_lon : offset + shift_lon + span_lon,
            offset + shift_lat : offset + shift_lat + span_lat,
        ]

    east_weight = window(east_edges, 0, 0)
    west_weight = window(east_edges, -1, 0)
    north_weight = window(north_edges, 0, 0)
    south_weight = window(north_edges, 0, -1)
    center_term = window(kappa_wide, 0, 0) + east_weight + west_weight + north_weight + south_weight
    interior = (
        window(sea_wide, 0, 0),
        center_term,
        east_weight,
        west_weight,
        north_weight,
        south_weight,
        window(area_wide, 0, 0),
    )
    sketch_masked = sketch * sea_mask
    columns = jnp.concatenate([sketch_masked, sign_columns(probe_bits) * sea_mask], axis=0)
    sketch_count = sketch.shape[0]
    thickness = 1
    columns_wide = extend(columns, thickness)
    first_pass = operate(columns_wide, interior)
    scaled = first_pass * interior[6]
    second = operate(extend(scaled[:sketch_count], 1), interior)
    local_gram = pair_gram(first_pass, scaled)
    summed = mesh_sum(local_gram)
    cell_total = lax.axis_size("lon") * lon_count * lax.axis_size("lat") * lat_count
    return (second, summed / cell_total)


def solution(mesh):
    in_specs = (
        P(None, "lon", "lat"),
        P(None, "lon", "lat"),
        P("lon", "lat"),
        P("lon", "lat"),
        P("lon", "lat"),
        P("lon", "lat"),
        P("lon", "lat"),
    )
    out_specs = (P(None, "lon", "lat"), P())
    return jax.shard_map(local, mesh=mesh, in_specs=in_specs, out_specs=out_specs, check_vma=False)
```

```python
import functools

import jax
import jax.numpy as jnp
from jax import lax
from jax.experimental import pallas as pl
from jax.experimental.pallas import tpu as pltpu
from jax.sharding import PartitionSpec as P

LANES = 128
BITS = 16
F32 = jnp.float32


def lane_ids(rows):
    return lax.broadcasted_iota(jnp.int32, (rows, LANES), 1)


def spread(words):
    shape = (BITS, words.shape[-1])
    shifts = lax.broadcasted_iota(jnp.int32, shape, 0)
    bits = jnp.bitwise_and(jnp.right_shift(jnp.broadcast_to(words, shape), shifts), 1)
    return (1 - 2 * bits).astype(F32)


def halves(field):
    return [field[:, h : h + LANES] for h in range(0, field.shape[-1], LANES)]


def lat_shifts(field, low_edge, high_edge):
    ids = lane_ids(field[0].shape[0])
    up = [pltpu.roll(part, LANES - 1, 1) for part in field] + [high_edge]
    down = [low_edge] + [pltpu.roll(part, 1, 1) for part in field]
    north = [jnp.where(ids == LANES - 1, up[h + 1], up[h]) for h in range(len(field))]
    south = [jnp.where(ids == 0, down[h], down[h + 1]) for h in range(len(field))]
    return north, south


def stencil(weights, middle, east, west, north, south):
    return [
        c * m - e * xe - w * xw - n * xn - s * xs
        for (c, e, w, n, s), m, xe, xw, xn, xs in zip(weights, middle, east, west, north, south)
    ]


def edge_at(edge, lane, target):
    return pltpu.roll(edge, (target - lane) % LANES, 1)


class Sizes:
    def __init__(self, sketch, probe_bits):
        self.count, self.lons, self.lats = sketch.shape
        self.words = probe_bits.shape[0]
        self.cols = self.count + BITS * self.words
        self.rows = -(-(self.count + self.words + 5) // 8) * 8
        self.edge_rows = -(-(self.count + 2) // 8) * 8
        self.lat_axis = lax.axis_size("lat")
        self.paired = self.lat_axis == 2


def edge_rows_of(sizes, low, high, lane, rows):
    if sizes.paired:
        first = lax.axis_index("lat") == 0
        picked = lax.select(first, high, low)
        shift = jnp.where(first, (lane + 1) % LANES, lane)
        return [pltpu.roll(picked, shift, 1)]
    return [pltpu.roll(low, lane, 1), pltpu.roll(high, (lane + 1) % LANES, 1)]


def pack_kernel(sizes, sk, wd, oc, ea, no, ka, ar, first_a, first_b, second_a, second_b, *edges):
    n, count = sizes.lons, sizes.count
    even = lax.rem(lax.axis_index("lon"), 2) == 0
    for first, second, ends in ((first_b, second_b, (0, n - 1)), (first_a, second_a, (n - 1, 0))):
        inner = tuple(1 if r == 0 else n - 2 for r in ends)

        def pick(get, where):
            return lax.select(even, get(where[0]), get(where[1]))

        first[0:count, :] = pick(lambda r: sk[:, r, :], ends)
        second[0:count, :] = pick(lambda r: sk[:, r, :], inner)
        for w in range(sizes.words):
            first[count + w : count + w + 1, :] = pick(lambda r: wd[w, r : r + 1, :], ends).astype(F32)
        base = count + sizes.words
        first[base : base + 1, :] = pick(lambda r: oc[r : r + 1, :], ends).astype(F32)
        for k, ref in enumerate((ea, no, ka, ar)):
            first[base + 1 + k : base + 2 + k, :] = pick(lambda r: ref[r : r + 1, :], ends)
        rest = first.shape[0] - base - 5
        if rest:
            first[base + 5 :, :] = jnp.zeros((rest, sizes.lats), F32)
        second[count : count + 1, :] = pick(lambda r: oc[r : r + 1, :], inner).astype(F32)
        second[count + 1 : count + 2, :] = pick(lambda r: ea[r : r + 1, :], inner)
        second[count + 2 :, :] = jnp.zeros((second.shape[0] - count - 2, sizes.lats), F32)

    last = sizes.lats - LANES
    for start in range(0, count, BITS):
        ids = lane_ids(BITS)
        total = [jnp.zeros((BITS, LANES), F32) for _ in edges]
        for i in range(n):
            low = sk[start : start + BITS, i, 0:LANES]
            high = sk[start : start + BITS, i, last:]
            moved = edge_rows_of(sizes, low, high, i, BITS)
            total = [jnp.where(ids == i, m, t) for m, t in zip(moved, total)]
        for edge, t in zip(edges, total):
            edge[start : start + BITS, :] = t

    def ends_of(at):
        parts = [wd[w, :, at : at + LANES].astype(F32) for w in range(sizes.words)]
        parts += [oc[:, at : at + LANES].astype(F32), no[:, at : at + LANES]]
        spare = LANES - n * len(parts)
        parts.append(jnp.zeros((spare, LANES), F32))
        return jnp.concatenate(parts, axis=0).T

    low, high = ends_of(0)[0:1, :], ends_of(last)[LANES - 1 :, :]
    if sizes.paired:
        rows = [lax.select(lax.axis_index("lat") == 0, high, low)]
    else:
        rows = [low, high]
    for edge, row in zip(edges, rows):
        edge[count:, :] = jnp.broadcast_to(row, (sizes.edge_rows - count, LANES))


def halo_rows(got_a, got_b, rows):
    even = lax.rem(lax.axis_index("lon"), 2) == 0
    a, b = got_a[rows, :], got_b[rows, :]
    return lax.select(even, b, a), lax.select(even, a, b)


def edge_columns(edge, sizes, index):
    row = edge[sizes.count : sizes.count + 1, :]
    turned = jnp.broadcast_to(row, (LANES, LANES)).T
    return turned[index * sizes.lons : (index + 1) * sizes.lons, 0:1]


def gram_kernel(
    sizes, sk, wd, oc, ea, no, ka, ar, got_a, got_b, got_low, got_high,
    gram, applied, coef, split_hi, split_lo, ext, root,
):
    n, count, lats, words = sizes.lons, sizes.count, sizes.lats, sizes.words
    base = count + words
    lat_id = lax.axis_index("lat")
    before, after = halo_rows(got_a, got_b, slice(base, base + 3))

    sea = oc[...].astype(F32)
    ext[0, 8 : 8 + n, :] = sea
    ext[0, 8 + n : 9 + n, :] = after[0:1]
    ext[1, 8 : 8 + n, :] = ea[...] * sea * ext[0, 9 : 9 + n, :]
    ext[1, 7:8, :] = before[1:2] * before[0:1] * sea[0:1]
    east_w = ext[1, 8 : 8 + n, :]
    west_w = ext[1, 7 : 7 + n, :]

    sea_low, north_low = (edge_columns(got_low, sizes, words + k) for k in (0, 1))
    sea_high = edge_columns(got_high, sizes, words)
    ids = lane_ids(n)
    sea_parts = halves(sea)
    half_north = [no[:, h * LANES : (h + 1) * LANES] * part for h, part in enumerate(sea_parts)]
    at_low = jnp.where(lat_id == 0, 0.0, 1.0)
    at_high = jnp.where(lat_id == sizes.lat_axis - 1, 0.0, 1.0)
    edge_high = jnp.broadcast_to(sea_high * at_high, (n, LANES))
    edge_low = jnp.broadcast_to(sea_low * north_low * at_low, (n, LANES))
    sea_north, _ = lat_shifts(sea_parts, edge_low, edge_high)
    _, flow_south = lat_shifts(half_north, edge_low, edge_high)
    north_w = jnp.concatenate([a * b for a, b in zip(half_north, sea_north)], axis=1)
    south_w = jnp.concatenate([a * b for a, b in zip(flow_south, sea_parts)], axis=1)
    coef[0] = sea * (ka[...] + east_w + west_w + north_w + south_w)
    coef[1] = east_w
    coef[2] = west_w
    coef[3] = north_w
    coef[4] = south_w
    root[...] = jnp.sqrt(ar[...])

    def weights_at(i):
        rows = [coef[k, i : i + 1, :] for k in range(5)]
        return list(zip(*[halves(r) for r in rows]))

    def one_block(start, get, low_edge, high_edge, keep):
        west, middle = get(-1), get(0)
        for i in range(n):
            east = get(i + 1)
            north, south = lat_shifts(
                middle, edge_at(low_edge, i, 0), edge_at(high_edge, i, LANES - 1)
            )
            out = stencil(weights_at(i), middle, east, west, north, south)
            for h, part in enumerate(out):
                if keep:
                    applied[i, pl.ds(start, BITS), h * LANES : (h + 1) * LANES] = part
                scaled = part * root[i : i + 1, h * LANES : (h + 1) * LANES]
                high = scaled.astype(jnp.bfloat16)
                at = slice(i * lats + h * LANES, i * lats + (h + 1) * LANES)
                split_hi[pl.ds(start, BITS), at] = high
                split_lo[pl.ds(start, BITS), at] = (scaled - high.astype(F32)).astype(jnp.bfloat16)
            west, middle = middle, east

    even = lax.rem(lax.axis_index("lon"), 2) == 0

    def sketch_block(k, carry):
        start = pl.multiple_of(k * BITS, BITS)
        rows = pl.ds(start, BITS)

        def get(i):
            if i == -1:
                return halves(lax.select(even, got_b[rows, :], got_a[rows, :]))
            if i == n:
                return halves(lax.select(even, got_a[rows, :], got_b[rows, :]))
            return halves(sk[rows, i, :])

        one_block(start, get, got_low[rows, :], got_high[rows, :], True)
        return carry

    lax.fori_loop(0, count // BITS, sketch_block, 0)
    for w in range(words):
        before_w, after_w = halo_rows(got_a, got_b, slice(count + w, count + w + 1))

        def get(i):
            if i == -1:
                row = before_w.astype(jnp.int32)
            elif i == n:
                row = after_w.astype(jnp.int32)
            else:
                row = wd[w, i : i + 1, :]
            return [spread(part) for part in halves(row)]

        edges = []
        for got in (got_low, got_high):
            row = got[count : count + 1, :].astype(jnp.int32)
            edges.append(spread(pltpu.roll(row, (LANES - w * n) % LANES, 1)))
        one_block(count + w * BITS, get, edges[0], edges[1], False)

    dims = (((1,), (1,)), ((), ()))
    main = lax.dot_general(split_hi[...], split_hi[...], dims, preferred_element_type=F32)
    cross = lax.dot_general(split_hi[...], split_lo[...], dims, preferred_element_type=F32)
    gram[...] = main + cross + cross.T


def edge_kernel(sizes, ar, got_a, got_b, applied, *edges):
    n, count, lats = sizes.lons, sizes.count, sizes.lats
    last = lats - LANES
    base = count + sizes.words
    even = lax.rem(lax.axis_index("lon"), 2) == 0

    def block(k, carry):
        start = pl.multiple_of(k * BITS, BITS)
        rows = pl.ds(start, BITS)
        ids = lane_ids(BITS)
        total = [jnp.zeros((BITS, LANES), F32) for _ in edges]
        for i in range(n + 2):
            if i < n:
                low = applied[i, rows, 0:LANES] * ar[i : i + 1, 0:LANES]
                high = applied[i, rows, last:] * ar[i : i + 1, last:]
            else:
                side = (got_b, got_a) if i == n else (got_a, got_b)
                low = lax.select(even, side[0][rows, 0:LANES], side[1][rows, 0:LANES])
                high = lax.select(even, side[0][rows, last:], side[1][rows, last:])
            moved = edge_rows_of(sizes, low, high, i, BITS)
            total = [jnp.where(ids == i, m, t) for m, t in zip(moved, total)]
        for edge, t in zip(edges, total):
            edge[rows, :] = t
        return carry

    lax.fori_loop(0, count // BITS, block, 0)
    tails = [jnp.zeros((8, LANES), F32) for _ in edges]
    ids, sub = lane_ids(8), lax.broadcasted_iota(jnp.int32, (8, LANES), 0)
    for k, row in enumerate((base, base + 2)):
        ends = halo_rows(got_a, got_b, slice(row, row + 1))
        for side, end in enumerate(ends):
            moved = edge_rows_of(
                sizes,
                jnp.broadcast_to(end[:, 0:LANES], (8, LANES)),
                jnp.broadcast_to(end[:, last:], (8, LANES)),
                n + side,
                8,
            )
            spot = (ids == n + side) & (sub == k)
            tails = [jnp.where(spot, m, t) for m, t in zip(moved, tails)]
    for edge, t in zip(edges, tails):
        edge[count : count + 8, :] = t


def image_kernel(
    sizes, sk, oc, ar, got_a, got_b, far_a, far_b, applied, coef, got_low, got_high, out,
):
    n, count, lats = sizes.lons, sizes.count, sizes.lats
    base = count + sizes.words
    even = lax.rem(lax.axis_index("lon"), 2) == 0
    lat_id = lax.axis_index("lat")
    at_low = jnp.where(lat_id == 0, 0.0, 1.0)
    at_high = jnp.where(lat_id == sizes.lat_axis - 1, 0.0, 1.0)
    near = halo_rows(got_a, got_b, slice(base, base + 5))
    far = halo_rows(far_a, far_b, slice(count, count + 2))
    ghost = []
    for side in (0, 1):
        rows = near[side]
        sea, east, north, kappa, area = (rows[k : k + 1] for k in range(5))
        if side == 0:
            east_w = coef[2, 0:1, :]
            west_w = far[0][1:2] * far[0][0:1] * sea
        else:
            east_w = east * sea * far[1][0:1]
            west_w = coef[1, n - 1 : n, :]
        lane = n + side
        low = got_low[count : count + 8, :]
        high = got_high[count : count + 8, :]
        edge_high = edge_at(high[0:1], lane, LANES - 1) * at_high
        edge_low = edge_at(low[0:1] * low[1:2], lane, 0) * at_low
        sea_parts = halves(sea)
        flow = halves(north * sea)
        sea_north, _ = lat_shifts(sea_parts, edge_low, edge_high)
        _, flow_south = lat_shifts(flow, edge_low, edge_high)
        north_w = jnp.concatenate([a * b for a, b in zip(flow, sea_north)], axis=1)
        south_w = jnp.concatenate([a * b for a, b in zip(flow_south, sea_parts)], axis=1)
        center = sea * (kappa + east_w + west_w + north_w + south_w)
        ghost.append(list(zip(*[halves(r * area) for r in (center, east_w, west_w, north_w, south_w)])))

    def weights_at(i):
        rows = [coef[k, i : i + 1, :] for k in range(5)]
        return list(zip(*[halves(r) for r in rows]))

    def block(k, carry):
        start = pl.multiple_of(k * BITS, BITS)
        rows = pl.ds(start, BITS)
        low_edge, high_edge = got_low[rows, :], got_high[rows, :]

        def pick(a, b):
            return halves(lax.select(even, a[rows, :], b[rows, :]))

        def get(i):
            if 0 <= i < n:
                return halves(applied[i, rows, :] * ar[i : i + 1, :])
            side = 0 if i < 0 else 1
            middle = pick(got_b, got_a) if side == 0 else pick(got_a, got_b)
            beyond = pick(far_b, far_a) if side == 0 else pick(far_a, far_b)
            inner = halves(sk[rows, 0 if side == 0 else n - 1, :])
            east, west = (inner, beyond) if side == 0 else (beyond, inner)
            north, south = lat_shifts(
                middle,
                edge_at(low_edge, n + side, 0),
                edge_at(high_edge, n + side, LANES - 1),
            )
            return stencil(ghost[side], middle, east, west, north, south)

        west, middle = get(-1), get(0)
        for i in range(n):
            east = get(i + 1)
            north, south = lat_shifts(
                middle, edge_at(low_edge, i, 0), edge_at(high_edge, i, LANES - 1)
            )
            parts = stencil(weights_at(i), middle, east, west, north, south)
            for h, part in enumerate(parts):
                out[rows, i, h * LANES : (h + 1) * LANES] = part
            west, middle = middle, east
        return carry

    lax.fori_loop(0, count // BITS, block, 0)


def call(kernel, sizes, outs, args, scratch=()):
    vmem = pl.BlockSpec(memory_space=pltpu.VMEM)
    return pl.pallas_call(
        functools.partial(kernel, sizes),
        out_shape=[jax.ShapeDtypeStruct(shape, F32) for shape in outs],
        in_specs=[vmem] * len(args),
        out_specs=[vmem] * len(outs),
        scratch_shapes=list(scratch),
    )(*args)


def mesh_sum(part):
    lons, lats = lax.axis_size("lon"), lax.axis_size("lat")
    if lons & (lons - 1) or lats & (lats - 1):
        return lax.psum(part, ("lon", "lat"))
    step = 1
    while step < lats:
        part = part + lax.ppermute(part, "lat", [(i, i ^ step) for i in range(lats)])
        step *= 2
    step = 1
    while step < lons:
        pairs = [
            (i * lats + j, (i ^ step) * lats + (lats - 1 - j)) for i in range(lons) for j in range(lats)
        ]
        part = part + lax.ppermute(part, ("lon", "lat"), pairs)
        step *= 2
    return part


def swap_edges(edges):
    count = lax.axis_size("lat")
    if len(edges) == 1:
        got = lax.ppermute(edges[0], "lat", [(0, 1), (1, 0)])
        return got, got
    low, high = edges
    from_low = lax.ppermute(high, "lat", [(i, (i + 1) % count) for i in range(count)])
    from_high = lax.ppermute(low, "lat", [((i + 1) % count, i) for i in range(count)])
    return from_low, from_high


def local(sketch, probe_bits, ocean, east_cond, north_cond, kappa_sq, inv_area):
    sizes = Sizes(sketch, probe_bits)
    n, lats, count = sizes.lons, sizes.lats, sizes.count
    lon_axis = lax.axis_size("lon")
    pairs_a = [(i, i ^ 1) for i in range(lon_axis)]
    pairs_b = [(i, (i + 1) % lon_axis if i % 2 else (i - 1) % lon_axis) for i in range(lon_axis)]
    fields = (sketch, probe_bits, ocean, east_cond, north_cond, kappa_sq, inv_area)
    line, far_line = (sizes.rows, lats), (sizes.edge_rows, lats)
    edge = (sizes.edge_rows, LANES)
    edge_count = 1 if sizes.paired else 2

    packed = call(pack_kernel, sizes, [line, line, far_line, far_line] + [edge] * edge_count, fields)
    first_a, first_b, second_a, second_b = packed[:4]
    got_b = lax.ppermute(first_b, "lon", pairs_b)
    got_a = lax.ppermute(first_a, "lon", pairs_a)
    low, high = swap_edges(packed[4:])
    far_b = lax.ppermute(second_b, "lon", pairs_b)
    far_a = lax.ppermute(second_a, "lon", pairs_a)

    gram, applied, coef = call(
        gram_kernel,
        sizes,
        [(sizes.cols, sizes.cols), (n, count, lats), (5, n, lats)],
        fields + (got_a, got_b, low, high),
        [
            pltpu.VMEM((sizes.cols, n * lats), jnp.bfloat16),
            pltpu.VMEM((sizes.cols, n * lats), jnp.bfloat16),
            pltpu.VMEM((2, n + 16, lats), F32),
            pltpu.VMEM((n, lats), F32),
        ],
    )
    edges = call(edge_kernel, sizes, [edge] * edge_count, (inv_area, got_a, got_b, applied))
    low2, high2 = swap_edges(edges)
    (image,) = call(
        image_kernel,
        sizes,
        [sketch.shape],
        (sketch, ocean, inv_area, got_a, got_b, far_a, far_b, applied, coef, low2, high2),
    )
    cells = lon_axis * n * sizes.lat_axis * lats
    return image, mesh_sum(gram) / cells


def solution(mesh):
    field, flat = P(None, "lon", "lat"), P("lon", "lat")
    return jax.shard_map(
        local,
        mesh=mesh,
        in_specs=(field, field, flat, flat, flat, flat, flat),
        out_specs=(field, P()),
        check_vma=False,
    )
```

```python
import functools

import jax
import jax.numpy as jnp
from jax import lax
from jax.experimental import pallas as pl
from jax.experimental.pallas import tpu as pltpu
from jax.sharding import PartitionSpec as P


LANES = 128
BITS = 16
F32 = jnp.float32


def lane_ids(rows):
    return lax.broadcasted_iota(jnp.int32, (rows, LANES), 1)


def spread(words):
    shape = (BITS, words.shape[-1])
    shifts = lax.broadcasted_iota(jnp.int32, shape, 0)
    bits = jnp.bitwise_and(jnp.right_shift(jnp.broadcast_to(words, shape), shifts), 1)
    return (1 - 2 * bits).astype(F32)


def halves(field):
    return [field[:, h : h + LANES] for h in range(0, field.shape[-1], LANES)]


def lat_shifts(field, low_edge, high_edge):
    ids = lane_ids(field[0].shape[0])
    up = [pltpu.roll(part, LANES - 1, 1) for part in field] + [high_edge]
    down = [low_edge] + [pltpu.roll(part, 1, 1) for part in field]
    north = [jnp.where(ids == LANES - 1, up[h + 1], up[h]) for h in range(len(field))]
    south = [jnp.where(ids == 0, down[h], down[h + 1]) for h in range(len(field))]
    return north, south


def stencil(weights, middle, east, west, north, south):
    return [
        c * m - e * xe - w * xw - n * xn - s * xs
        for (c, e, w, n, s), m, xe, xw, xn, xs in zip(weights, middle, east, west, north, south)
    ]


def edge_at(edge, lane, target):
    return pltpu.roll(edge, (target - lane) % LANES, 1)


class Sizes:
    def __init__(self, sketch, probe_bits):
        self.count, self.lons, self.lats = sketch.shape
        self.words = probe_bits.shape[0]
        self.cols = self.count + BITS * self.words
        self.rows = -(-(self.count + self.words + 5) // 8) * 8
        self.edge_rows = -(-(self.count + 2) // 8) * 8
        self.lat_axis = lax.axis_size("lat")
        self.paired = self.lat_axis == 2
        self.folded = 4 * self.cols == 3 * LANES and self.cols % 48 == 0
        self.cells = lax.axis_size("lon") * self.lons * self.lat_axis * self.lats


def edge_rows_of(sizes, low, high, lane):
    if sizes.paired:
        first = lax.axis_index("lat") == 0
        picked = lax.select(first, high, low)
        shift = jnp.where(first, (lane + 1) % LANES, lane)
        return [pltpu.roll(picked, shift, 1)]
    return [pltpu.roll(low, lane, 1), pltpu.roll(high, (lane + 1) % LANES, 1)]


def end_row(sizes, sk, wd, oc, fields, first, r):
    count, base = sizes.count, sizes.count + sizes.words
    first[0:count, :] = sk[:, r, :]
    for w in range(sizes.words):
        first[count + w : count + w + 1, :] = wd[w, r : r + 1, :].astype(F32)
    first[base : base + 1, :] = oc[r : r + 1, :].astype(F32)
    for k, ref in enumerate(fields):
        first[base + 1 + k : base + 2 + k, :] = ref[r : r + 1, :]
    rest = first.shape[0] - base - 5
    if rest:
        first[base + 5 :, :] = jnp.zeros((rest, sizes.lats), F32)


def load_kernel(sizes, *refs):
    given, held, rows, sems = refs[:7], refs[7:14], refs[14:18], refs[18]
    n, count = sizes.lons, sizes.count
    copies = [pltpu.make_async_copy(g, h, sems.at[k]) for k, (g, h) in enumerate(zip(given, held))]
    for copy in copies:
        copy.start()
    for copy in copies:
        copy.wait()
    sk, wd, oc, ea = held[:4]
    for ref, r in zip(rows[:2], (n - 1, 0)):
        end_row(sizes, sk, wd, oc, held[3:], ref, r)
    for ref, r in zip(rows[2:], (n - 2, 1)):
        ref[0:count, :] = sk[:, r, :]
        ref[count : count + 1, :] = oc[r : r + 1, :].astype(F32)
        ref[count + 1 : count + 2, :] = ea[r : r + 1, :]
        ref[count + 2 :, :] = jnp.zeros((ref.shape[0] - count - 2, sizes.lats), F32)


def pack_kernel(sizes, sk, wd, oc, no, *edges):
    n, count = sizes.lons, sizes.count
    last = sizes.lats - LANES
    for start in range(0, count, BITS):
        ids = lane_ids(BITS)
        total = [jnp.zeros((BITS, LANES), F32) for _ in edges]
        for i in range(n):
            low = sk[start : start + BITS, i, 0:LANES]
            high = sk[start : start + BITS, i, last:]
            moved = edge_rows_of(sizes, low, high, i)
            total = [jnp.where(ids == i, m, t) for m, t in zip(moved, total)]
        for edge, t in zip(edges, total):
            edge[start : start + BITS, :] = t

    def ends_of(at):
        parts = [wd[w, :, at : at + LANES].astype(F32) for w in range(sizes.words)]
        parts += [oc[:, at : at + LANES].astype(F32), no[:, at : at + LANES]]
        spare = LANES - n * len(parts)
        parts.append(jnp.zeros((spare, LANES), F32))
        return jnp.concatenate(parts, axis=0).T

    low, high = ends_of(0)[0:1, :], ends_of(last)[LANES - 1 :, :]
    if sizes.paired:
        rows = [lax.select(lax.axis_index("lat") == 0, high, low)]
    else:
        rows = [low, high]
    for edge, row in zip(edges, rows):
        edge[count:, :] = jnp.broadcast_to(row, (sizes.edge_rows - count, LANES))


def edge_columns(edge, sizes, index):
    row = edge[sizes.count : sizes.count + 1, :]
    turned = jnp.broadcast_to(row, (LANES, LANES)).T
    return turned[index * sizes.lons : (index + 1) * sizes.lons, 0:1]


def gram_kernel(
    sizes, sk, wd, oc, ea, no, ka, ar, west_row, east_row, got_low, got_high,
    gram, applied, coef, split_hi, split_lo, ext, root, whole,
):
    n, count, lats, words = sizes.lons, sizes.count, sizes.lats, sizes.words
    base = count + words
    lat_id = lax.axis_index("lat")
    before, after = west_row[base : base + 3, :], east_row[base : base + 1, :]

    sea = oc[...].astype(F32)
    ext[0, 8 : 8 + n, :] = sea
    ext[0, 8 + n : 9 + n, :] = after[0:1]
    ext[1, 8 : 8 + n, :] = ea[...] * sea * ext[0, 9 : 9 + n, :]
    ext[1, 7:8, :] = before[1:2] * before[0:1] * sea[0:1]
    east_w = ext[1, 8 : 8 + n, :]
    west_w = ext[1, 7 : 7 + n, :]

    sea_low, north_low = (edge_columns(got_low, sizes, words + k) for k in (0, 1))
    sea_high = edge_columns(got_high, sizes, words)
    ids = lane_ids(n)
    sea_parts = halves(sea)
    half_north = [no[:, h * LANES : (h + 1) * LANES] * part for h, part in enumerate(sea_parts)]
    at_low = jnp.where(lat_id == 0, 0.0, 1.0)
    at_high = jnp.where(lat_id == sizes.lat_axis - 1, 0.0, 1.0)
    edge_high = jnp.broadcast_to(sea_high * at_high, (n, LANES))
    edge_low = jnp.broadcast_to(sea_low * north_low * at_low, (n, LANES))
    sea_north, _ = lat_shifts(sea_parts, edge_low, edge_high)
    _, flow_south = lat_shifts(half_north, edge_low, edge_high)
    north_w = jnp.concatenate([a * b for a, b in zip(half_north, sea_north)], axis=1)
    south_w = jnp.concatenate([a * b for a, b in zip(flow_south, sea_parts)], axis=1)
    coef[0] = sea * (ka[...] + east_w + west_w + north_w + south_w)
    coef[1] = east_w
    coef[2] = west_w
    coef[3] = north_w
    coef[4] = south_w
    root[...] = jnp.sqrt(ar[...])

    def weights_at(i):
        rows = [coef[k, i : i + 1, :] for k in range(5)]
        return list(zip(*[halves(r) for r in rows]))

    def one_block(start, get, low_edge, high_edge, keep):
        west, middle = get(-1), get(0)
        for i in range(n):
            east = get(i + 1)
            north, south = lat_shifts(
                middle, edge_at(low_edge, i, 0), edge_at(high_edge, i, LANES - 1)
            )
            out = stencil(weights_at(i), middle, east, west, north, south)
            for h, part in enumerate(out):
                if keep:
                    applied[i, pl.ds(start, BITS), h * LANES : (h + 1) * LANES] = part
                scaled = part * root[i : i + 1, h * LANES : (h + 1) * LANES]
                high = scaled.astype(jnp.bfloat16)
                at = slice(i * lats + h * LANES, i * lats + (h + 1) * LANES)
                split_hi[pl.ds(start, BITS), at] = high
                split_lo[pl.ds(start, BITS), at] = (scaled - high.astype(F32)).astype(jnp.bfloat16)
            west, middle = middle, east

    def sketch_block(k, carry):
        start = pl.multiple_of(k * BITS, BITS)
        rows = pl.ds(start, BITS)

        def get(i):
            if i == -1:
                return halves(west_row[rows, :])
            if i == n:
                return halves(east_row[rows, :])
            return halves(sk[rows, i, :])

        one_block(start, get, got_low[rows, :], got_high[rows, :], True)
        return carry

    lax.fori_loop(0, count // BITS, sketch_block, 0)
    for w in range(words):
        before_w, after_w = (ref[count + w : count + w + 1, :] for ref in (west_row, east_row))

        def get(i):
            if i == -1:
                row = before_w.astype(jnp.int32)
            elif i == n:
                row = after_w.astype(jnp.int32)
            else:
                row = wd[w, i : i + 1, :]
            return [spread(part) for part in halves(row)]

        edges = []
        for got in (got_low, got_high):
            row = got[count : count + 1, :].astype(jnp.int32)
            edges.append(spread(pltpu.roll(row, (LANES - w * n) % LANES, 1)))
        one_block(count + w * BITS, get, edges[0], edges[1], False)

    dims = (((1,), (1,)), ((), ()))
    main = lax.dot_general(split_hi[...], split_hi[...], dims, preferred_element_type=F32)
    cross = lax.dot_general(split_hi[...], split_lo[...], dims, preferred_element_type=F32)
    total = main + cross + cross.T
    if not sizes.folded:
        gram[...] = total
        return
    block, short = sizes.cols // 3, sizes.cols // 6
    whole[:, 0 : sizes.cols] = total
    rows = [whole[k * short : (k + 1) * short, :] for k in range(6)]
    ids = lane_ids(block)
    gram[0:block, :] = jnp.where(ids < sizes.cols, whole[0:block, :], pltpu.roll(whole[block : 2 * block, :], 2 * block, 1))
    ids = lane_ids(short) // block
    moved = [pltpu.roll(rows[2], 2 * block, 1), pltpu.roll(rows[3], 3 * block, 1), rows[4], pltpu.roll(rows[5], block, 1)]
    gram[block:, :] = jnp.where(ids == 0, moved[0], jnp.where(ids == 1, moved[1], jnp.where(ids == 2, moved[2], moved[3])))


def unfold_kernel(sizes, mine, other, out):
    total = (mine[...] + other[...]) / sizes.cells
    if not sizes.folded:
        out[...] = total
        return
    block = sizes.cols // 3
    top, low = total[0:block, :], total[block:, :]
    ids = lane_ids(block)
    middle = jnp.concatenate([pltpu.roll(low, 2 * block, 1), pltpu.roll(low, block, 1)], axis=0)
    second = jnp.where(ids < 2 * block, pltpu.roll(top, 2 * block, 1), middle)
    third = jnp.concatenate([low, pltpu.roll(low, 3 * block, 1)], axis=0)
    upper = jnp.concatenate([top, second, third, jnp.zeros((block, LANES), F32)], axis=0)
    across = lane_ids(LANES) // block
    down = lax.broadcasted_iota(jnp.int32, (LANES, LANES), 0) // block
    out[...] = jnp.where(down <= across, upper, upper.T)[0 : sizes.cols, 0 : sizes.cols]


def edge_kernel(sizes, ar, west_row, east_row, applied, *edges):
    n, count, lats = sizes.lons, sizes.count, sizes.lats
    last = lats - LANES
    base = count + sizes.words

    def block(k, carry):
        start = pl.multiple_of(k * BITS, BITS)
        rows = pl.ds(start, BITS)
        ids = lane_ids(BITS)
        total = [jnp.zeros((BITS, LANES), F32) for _ in edges]
        for i in range(n + 2):
            if i < n:
                low = applied[i, rows, 0:LANES] * ar[i : i + 1, 0:LANES]
                high = applied[i, rows, last:] * ar[i : i + 1, last:]
            else:
                side = west_row if i == n else east_row
                low, high = side[rows, 0:LANES], side[rows, last:]
            moved = edge_rows_of(sizes, low, high, i)
            total = [jnp.where(ids == i, m, t) for m, t in zip(moved, total)]
        for edge, t in zip(edges, total):
            edge[rows, :] = t
        return carry

    lax.fori_loop(0, count // BITS, block, 0)
    tails = [jnp.zeros((8, LANES), F32) for _ in edges]
    ids, sub = lane_ids(8), lax.broadcasted_iota(jnp.int32, (8, LANES), 0)
    for k, row in enumerate((base, base + 2)):
        ends = [ref[row : row + 1, :] for ref in (west_row, east_row)]
        for side, end in enumerate(ends):
            moved = edge_rows_of(
                sizes,
                jnp.broadcast_to(end[:, 0:LANES], (8, LANES)),
                jnp.broadcast_to(end[:, last:], (8, LANES)),
                n + side,
            )
            spot = (ids == n + side) & (sub == k)
            tails = [jnp.where(spot, m, t) for m, t in zip(moved, tails)]
    for edge, t in zip(edges, tails):
        edge[count : count + 8, :] = t


def image_kernel(
    sizes, sk, oc, ar, west_row, east_row, far_west, far_east, applied, coef, got_low, got_high, out,
):
    n, count = sizes.lons, sizes.count
    base = count + sizes.words
    lat_id = lax.axis_index("lat")
    at_low = jnp.where(lat_id == 0, 0.0, 1.0)
    at_high = jnp.where(lat_id == sizes.lat_axis - 1, 0.0, 1.0)
    near = [ref[base : base + 5, :] for ref in (west_row, east_row)]
    far = [ref[count : count + 2, :] for ref in (far_west, far_east)]
    ghost = []
    for side in (0, 1):
        rows = near[side]
        sea, east, north, kappa, area = (rows[k : k + 1] for k in range(5))
        if side == 0:
            east_w = coef[2, 0:1, :]
            west_w = far[0][1:2] * far[0][0:1] * sea
        else:
            east_w = east * sea * far[1][0:1]
            west_w = coef[1, n - 1 : n, :]
        lane = n + side
        low = got_low[count : count + 8, :]
        high = got_high[count : count + 8, :]
        edge_high = edge_at(high[0:1], lane, LANES - 1) * at_high
        edge_low = edge_at(low[0:1] * low[1:2], lane, 0) * at_low
        sea_parts = halves(sea)
        flow = halves(north * sea)
        sea_north, _ = lat_shifts(sea_parts, edge_low, edge_high)
        _, flow_south = lat_shifts(flow, edge_low, edge_high)
        north_w = jnp.concatenate([a * b for a, b in zip(flow, sea_north)], axis=1)
        south_w = jnp.concatenate([a * b for a, b in zip(flow_south, sea_parts)], axis=1)
        center = sea * (kappa + east_w + west_w + north_w + south_w)
        ghost.append(list(zip(*[halves(r * area) for r in (center, east_w, west_w, north_w, south_w)])))

    def weights_at(i):
        rows = [coef[k, i : i + 1, :] for k in range(5)]
        return list(zip(*[halves(r) for r in rows]))

    def block(k, carry):
        start = pl.multiple_of(k * BITS, BITS)
        rows = pl.ds(start, BITS)
        low_edge, high_edge = got_low[rows, :], got_high[rows, :]

        def get(i):
            if 0 <= i < n:
                return halves(applied[i, rows, :] * ar[i : i + 1, :])
            side = 0 if i < 0 else 1
            middle = halves((west_row, east_row)[side][rows, :])
            beyond = halves((far_west, far_east)[side][rows, :])
            inner = halves(sk[rows, 0 if side == 0 else n - 1, :])
            east, west = (inner, beyond) if side == 0 else (beyond, inner)
            north, south = lat_shifts(
                middle,
                edge_at(low_edge, n + side, 0),
                edge_at(high_edge, n + side, LANES - 1),
            )
            return stencil(ghost[side], middle, east, west, north, south)

        west, middle = get(-1), get(0)
        for i in range(n):
            east = get(i + 1)
            north, south = lat_shifts(
                middle, edge_at(low_edge, i, 0), edge_at(high_edge, i, LANES - 1)
            )
            parts = stencil(weights_at(i), middle, east, west, north, south)
            for h, part in enumerate(parts):
                out[rows, i, h * LANES : (h + 1) * LANES] = part
            west, middle = middle, east
        return carry

    lax.fori_loop(0, count // BITS, block, 0)


def call(kernel, sizes, outs, args, scratch=(), inputs=pltpu.VMEM, limit=16 << 20):
    outs = [o if isinstance(o, jax.ShapeDtypeStruct) else jax.ShapeDtypeStruct(o, F32) for o in outs]
    vmem = pl.BlockSpec(memory_space=pltpu.VMEM)
    return pl.pallas_call(
        functools.partial(kernel, sizes),
        out_shape=outs,
        in_specs=[pl.BlockSpec(memory_space=inputs)] * len(args),
        out_specs=[vmem] * len(outs),
        scratch_shapes=list(scratch),
        compiler_params=pltpu.CompilerParams(vmem_limit_bytes=limit),
    )(*args)


def exchanges():
    lons, lats = lax.axis_size("lon"), lax.axis_size("lat")
    steps = [[(i * lats + j, i * lats + (j ^ bit)) for i in range(lons) for j in range(lats)] for bit in powers(lats)]
    steps += [
        [(i * lats + j, (i ^ bit) * lats + (lats - 1 - j)) for i in range(lons) for j in range(lats)]
        for bit in powers(lons)
    ]
    return steps


def powers(limit):
    return [1 << k for k in range(limit.bit_length() - 1)]


def swap_edges(edges):
    count = lax.axis_size("lat")
    if len(edges) == 1:
        got = lax.ppermute(edges[0], "lat", [(0, 1), (1, 0)])
        return got, got
    low, high = edges
    from_low = lax.ppermute(high, "lat", [(i, (i + 1) % count) for i in range(count)])
    from_high = lax.ppermute(low, "lat", [((i + 1) % count, i) for i in range(count)])
    return from_low, from_high


def local(sketch, probe_bits, ocean, east_cond, north_cond, kappa_sq, inv_area):
    sizes = Sizes(sketch, probe_bits)
    n, lats, count = sizes.lons, sizes.lats, sizes.count
    lon_axis = lax.axis_size("lon")
    eastward = [(i, (i + 1) % lon_axis) for i in range(lon_axis)]
    westward = [((i + 1) % lon_axis, i) for i in range(lon_axis)]
    fields = (sketch, probe_bits, ocean, east_cond, north_cond, kappa_sq, inv_area)
    line, far_line = (sizes.rows, lats), (sizes.edge_rows, lats)
    edge = (sizes.edge_rows, LANES)
    edge_count = 1 if sizes.paired else 2

    shapes = [jax.ShapeDtypeStruct(f.shape, f.dtype) for f in fields]
    *fields, to_east, to_west, far_to_east, far_to_west = call(
        load_kernel,
        sizes,
        shapes + [line, line, far_line, far_line],
        [pltpu.with_memory_space_constraint(f, pltpu.HBM) for f in fields],
        [pltpu.SemaphoreType.DMA((7,))],
        inputs=pltpu.HBM,
    )
    fields = tuple(fields)
    sketch, probe_bits, ocean, _, north_cond, _, inv_area = fields
    west_row = lax.ppermute(to_east, "lon", eastward)
    east_row = lax.ppermute(to_west, "lon", westward)
    far_east = lax.ppermute(far_to_west, "lon", westward)
    packed = call(pack_kernel, sizes, [edge] * edge_count, (sketch, probe_bits, ocean, north_cond))
    low, high = swap_edges(packed)
    far_west = lax.ppermute(far_to_east, "lon", eastward)

    gram, applied, coef = call(
        gram_kernel,
        sizes,
        [(sizes.cols // 2, LANES) if sizes.folded else (sizes.cols, sizes.cols), (n, count, lats), (5, n, lats)],
        fields + (west_row, east_row, low, high),
        [
            pltpu.VMEM((sizes.cols, n * lats), jnp.bfloat16),
            pltpu.VMEM((sizes.cols, n * lats), jnp.bfloat16),
            pltpu.VMEM((2, n + 16, lats), F32),
            pltpu.VMEM((n, lats), F32),
            pltpu.VMEM((sizes.cols, LANES), F32),
        ],
    )
    edges = call(edge_kernel, sizes, [edge] * edge_count, (inv_area, west_row, east_row, applied))
    low2, high2 = swap_edges(edges)
    (image,) = call(
        image_kernel,
        sizes,
        [sketch.shape],
        (sketch, ocean, inv_area, west_row, east_row, far_west, far_east, applied, coef, low2, high2),
    )
    steps = exchanges()
    for k, pairs in enumerate(steps):
        other = lax.ppermute(gram, ("lon", "lat"), pairs)
        if k < len(steps) - 1:
            gram = gram + other
    (gram,) = call(unfold_kernel, sizes, [(sizes.cols, sizes.cols)], (gram, other))
    return image, gram


def solution(mesh):
    field, flat = P(None, "lon", "lat"), P("lon", "lat")
    return jax.shard_map(
        local,
        mesh=mesh,
        in_specs=(field, field, flat, flat, flat, flat, flat),
        out_specs=(field, P()),
        check_vma=False,
    )
```

```python
import functools

import jax
import jax.numpy as jnp
from jax import lax
from jax.experimental import pallas as pl
from jax.experimental.pallas import tpu as pltpu
from jax.sharding import PartitionSpec as P


LANES = 128
BITS = 16
F32 = jnp.float32


def lane_ids(rows):
    return lax.broadcasted_iota(jnp.int32, (rows, LANES), 1)


def spread(words):
    shape = (BITS, words.shape[-1])
    shifts = lax.broadcasted_iota(jnp.int32, shape, 0)
    bits = jnp.bitwise_and(jnp.right_shift(jnp.broadcast_to(words, shape), shifts), 1)
    return (1 - 2 * bits).astype(F32)


def halves(field):
    return [field[:, h : h + LANES] for h in range(0, field.shape[-1], LANES)]


def lat_shifts(field, low_edge, high_edge):
    ids = lane_ids(field[0].shape[0])
    up = [pltpu.roll(part, LANES - 1, 1) for part in field] + [high_edge]
    down = [low_edge] + [pltpu.roll(part, 1, 1) for part in field]
    north = [jnp.where(ids == LANES - 1, up[h + 1], up[h]) for h in range(len(field))]
    south = [jnp.where(ids == 0, down[h], down[h + 1]) for h in range(len(field))]
    return north, south


def stencil(weights, middle, east, west, north, south):
    return [
        c * m - e * xe - w * xw - n * xn - s * xs
        for (c, e, w, n, s), m, xe, xw, xn, xs in zip(weights, middle, east, west, north, south)
    ]


def edge_at(edge, lane, target):
    return pltpu.roll(edge, (target - lane) % LANES, 1)


class Sizes:
    def __init__(self, sketch, probe_bits):
        self.count, self.lons, self.lats = sketch.shape
        self.words = probe_bits.shape[0]
        self.cols = self.count + BITS * self.words
        self.rows = -(-(self.count + self.words + 5) // 8) * 8
        self.edge_rows = -(-(self.count + 2) // 8) * 8
        self.lat_axis = lax.axis_size("lat")
        self.paired = self.lat_axis == 2
        self.folded = 4 * self.cols == 3 * LANES and self.cols % 48 == 0
        self.cells = lax.axis_size("lon") * self.lons * self.lat_axis * self.lats


def edge_rows_of(sizes, low, high, lane):
    if sizes.paired:
        first = lax.axis_index("lat") == 0
        picked = lax.select(first, high, low)
        shift = jnp.where(first, (lane + 1) % LANES, lane)
        return [pltpu.roll(picked, shift, 1)]
    return [pltpu.roll(low, lane, 1), pltpu.roll(high, (lane + 1) % LANES, 1)]


def end_row(sizes, sk, wd, oc, fields, first, r):
    count, base = sizes.count, sizes.count + sizes.words
    first[0:count, :] = sk[:, r, :]
    for w in range(sizes.words):
        first[count + w : count + w + 1, :] = wd[w, r : r + 1, :].astype(F32)
    first[base : base + 1, :] = oc[r : r + 1, :].astype(F32)
    for k, ref in enumerate(fields):
        first[base + 1 + k : base + 2 + k, :] = ref[r : r + 1, :]
    rest = first.shape[0] - base - 5
    if rest:
        first[base + 5 :, :] = jnp.zeros((rest, sizes.lats), F32)


def load_kernel(sizes, *refs):
    given, held, rows, edges, sems = refs[:7], refs[7:14], refs[14:18], refs[18:-1], refs[-1]
    n, count = sizes.lons, sizes.count
    copies = [pltpu.make_async_copy(g, h, sems.at[k]) for k, (g, h) in enumerate(zip(given, held))]
    for copy in copies:
        copy.start()
    for copy in copies:
        copy.wait()
    sk, wd, oc, ea = held[:4]
    for ref, r in zip(rows[:2], (n - 1, 0)):
        end_row(sizes, sk, wd, oc, held[3:], ref, r)
    for ref, r in zip(rows[2:], (n - 2, 1)):
        ref[0:count, :] = sk[:, r, :]
        ref[count : count + 1, :] = oc[r : r + 1, :].astype(F32)
        ref[count + 1 : count + 2, :] = ea[r : r + 1, :]
        ref[count + 2 :, :] = jnp.zeros((ref.shape[0] - count - 2, sizes.lats), F32)


    no = held[4]
    last = sizes.lats - LANES
    for start in range(0, count, BITS):
        ids = lane_ids(BITS)
        total = [jnp.zeros((BITS, LANES), F32) for _ in edges]
        for i in range(n):
            low = sk[start : start + BITS, i, 0:LANES]
            high = sk[start : start + BITS, i, last:]
            moved = edge_rows_of(sizes, low, high, i)
            total = [jnp.where(ids == i, m, t) for m, t in zip(moved, total)]
        for edge, t in zip(edges, total):
            edge[start : start + BITS, :] = t

    def ends_of(at):
        parts = [wd[w, :, at : at + LANES].astype(F32) for w in range(sizes.words)]
        parts += [oc[:, at : at + LANES].astype(F32), no[:, at : at + LANES]]
        spare = LANES - n * len(parts)
        parts.append(jnp.zeros((spare, LANES), F32))
        return jnp.concatenate(parts, axis=0).T

    low, high = ends_of(0)[0:1, :], ends_of(last)[LANES - 1 :, :]
    if sizes.paired:
        rows = [lax.select(lax.axis_index("lat") == 0, high, low)]
    else:
        rows = [low, high]
    for edge, row in zip(edges, rows):
        edge[count:, :] = jnp.broadcast_to(row, (sizes.edge_rows - count, LANES))


def edge_columns(edge, sizes, index):
    row = edge[sizes.count : sizes.count + 1, :]
    turned = jnp.broadcast_to(row, (LANES, LANES)).T
    return turned[index * sizes.lons : (index + 1) * sizes.lons, 0:1]


def far_side():
    return lax.axis_index("lon") == lax.axis_size("lon") - 1


def products(split_hi, split_lo):
    dims = (((1,), (1,)), ((), ()))
    main = lax.dot_general(split_hi[...], split_hi[...], dims, preferred_element_type=F32)
    cross = lax.dot_general(split_hi[...], split_lo[...], dims, preferred_element_type=F32)
    return main + cross + cross.T


def store_split(split_hi, split_lo, rows, at, scaled):
    high = scaled.astype(jnp.bfloat16)
    split_hi[rows, at] = high
    split_lo[rows, at] = (scaled - high.astype(F32)).astype(jnp.bfloat16)


def rows_of(refs, where):
    return list(zip(*[halves(refs[(k,) + where]) for k in range(5)]))


def probe_edges(sizes, w, got_low, got_high):
    edges = []
    for got in (got_low, got_high):
        row = got[sizes.count : sizes.count + 1, :].astype(jnp.int32)
        edges.append(spread(pltpu.roll(row, (LANES - w * sizes.lons) % LANES, 1)))
    return edges


def inner_kernel(
    far, sizes, sk, wd, oc, ea, no, ka, ar, got_low, got_high,
    applied, coef, partial, split_hi, split_lo, ext, root,
):
    n, count, lats, words = sizes.lons, sizes.count, sizes.lats, sizes.words

    @pl.when(far_side() == far)
    def _():
        lat_id = lax.axis_index("lat")
        sea = oc[...].astype(F32)
        ext[0, 8 : 8 + n, :] = sea
        ext[0, 8 + n : 9 + n, :] = jnp.zeros((1, lats), F32)
        ext[1, 8 : 8 + n, :] = ea[...] * sea * ext[0, 9 : 9 + n, :]
        ext[1, 7:8, :] = jnp.zeros((1, lats), F32)
        east_w = ext[1, 8 : 8 + n, :]
        west_w = ext[1, 7 : 7 + n, :]

        sea_low, north_low = (edge_columns(got_low, sizes, words + k) for k in (0, 1))
        sea_high = edge_columns(got_high, sizes, words)
        sea_parts = halves(sea)
        half_north = [no[:, h * LANES : (h + 1) * LANES] * part for h, part in enumerate(sea_parts)]
        at_low = jnp.where(lat_id == 0, 0.0, 1.0)
        at_high = jnp.where(lat_id == sizes.lat_axis - 1, 0.0, 1.0)
        edge_high = jnp.broadcast_to(sea_high * at_high, (n, LANES))
        edge_low = jnp.broadcast_to(sea_low * north_low * at_low, (n, LANES))
        sea_north, _ = lat_shifts(sea_parts, edge_low, edge_high)
        _, flow_south = lat_shifts(half_north, edge_low, edge_high)
        north_w = jnp.concatenate([a * b for a, b in zip(half_north, sea_north)], axis=1)
        south_w = jnp.concatenate([a * b for a, b in zip(flow_south, sea_parts)], axis=1)
        coef[0] = sea * (ka[...] + east_w + west_w + north_w + south_w)
        coef[1] = east_w
        coef[2] = west_w
        coef[3] = north_w
        coef[4] = south_w
        root[...] = jnp.sqrt(ar[...])

        def one_block(start, get, low_edge, high_edge, keep):
            rows = pl.ds(start, BITS)
            west, middle = get(0), get(1)
            for i in range(1, n - 1):
                east = get(i + 1)
                north, south = lat_shifts(
                    middle, edge_at(low_edge, i, 0), edge_at(high_edge, i, LANES - 1)
                )
                weights = rows_of(coef, (slice(i, i + 1), slice(None)))
                for h, part in enumerate(stencil(weights, middle, east, west, north, south)):
                    here = slice(h * LANES, (h + 1) * LANES)
                    if keep:
                        applied[i - 1, rows, here] = part
                    at = slice((i - 1) * lats + h * LANES, (i - 1) * lats + (h + 1) * LANES)
                    store_split(split_hi, split_lo, rows, at, part * root[i : i + 1, here])
                west, middle = middle, east

        def sketch_block(k, carry):
            start = pl.multiple_of(k * BITS, BITS)
            rows = pl.ds(start, BITS)
            one_block(start, lambda i: halves(sk[rows, i, :]), got_low[rows, :], got_high[rows, :], True)
            return carry

        lax.fori_loop(0, count // BITS, sketch_block, 0)
        for w in range(words):
            one_block(
                count + w * BITS,
                lambda i: [spread(part) for part in halves(wd[w, i : i + 1, :])],
                *probe_edges(sizes, w, got_low, got_high),
                False,
            )
        partial[...] = products(split_hi, split_lo)


def gram_kernel(
    sizes, sk, wd, oc, ea, ka, ar, west_row, east_row, got_low, got_high,
    coef_near, coef_far, partial_near, partial_far,
    gram, ends, end_coef, split_hi, split_lo, whole,
):
    n, count, lats, words = sizes.lons, sizes.count, sizes.lats, sizes.words
    base = count + words
    far = far_side()

    def inner(k, i):
        return lax.select(far, coef_far[k, i : i + 1, :], coef_near[k, i : i + 1, :])

    root = []
    for side, i in enumerate((0, n - 1)):
        sea = oc[i : i + 1, :].astype(F32)
        east_w, west_w, north_w, south_w = (inner(k, i) for k in range(1, 5))
        if side == 0:
            west_w = west_row[base + 1 : base + 2, :] * west_row[base : base + 1, :] * sea
        else:
            east_w = ea[i : i + 1, :] * sea * east_row[base : base + 1, :]
        center = sea * (ka[i : i + 1, :] + east_w + west_w + north_w + south_w)
        for k, row in enumerate((center, east_w, west_w, north_w, south_w)):
            end_coef[k, side : side + 1, :] = row
        root.append(jnp.sqrt(ar[i : i + 1, :]))

    def one_block(start, get, low_edge, high_edge, keep):
        rows = pl.ds(start, BITS)
        for side, i in enumerate((0, n - 1)):
            middle = get(i)
            north, south = lat_shifts(middle, edge_at(low_edge, i, 0), edge_at(high_edge, i, LANES - 1))
            weights = rows_of(end_coef, (slice(side, side + 1), slice(None)))
            for h, part in enumerate(stencil(weights, middle, get(i + 1), get(i - 1), north, south)):
                here = slice(h * LANES, (h + 1) * LANES)
                if keep:
                    ends[side, rows, here] = part
                at = slice(side * lats + h * LANES, side * lats + (h + 1) * LANES)
                store_split(split_hi, split_lo, rows, at, part * root[side][:, here])

    for start in range(0, count, BITS):
        rows = slice(start, start + BITS)

        def get(i):
            if i == -1:
                return halves(west_row[rows, :])
            if i == n:
                return halves(east_row[rows, :])
            return halves(sk[rows, i, :])

        one_block(start, get, got_low[rows, :], got_high[rows, :], True)
    for w in range(words):

        def get(i):
            if i == -1:
                row = west_row[count + w : count + w + 1, :].astype(jnp.int32)
            elif i == n:
                row = east_row[count + w : count + w + 1, :].astype(jnp.int32)
            else:
                row = wd[w, i : i + 1, :]
            return [spread(part) for part in halves(row)]

        one_block(count + w * BITS, get, *probe_edges(sizes, w, got_low, got_high), False)

    total = lax.select(far, partial_far[...], partial_near[...]) + products(split_hi, split_lo)
    if not sizes.folded:
        gram[...] = total
        return
    block, short = sizes.cols // 3, sizes.cols // 6
    whole[:, 0 : sizes.cols] = total
    rows = [whole[k * short : (k + 1) * short, :] for k in range(6)]
    ids = lane_ids(block)
    gram[0:block, :] = jnp.where(ids < sizes.cols, whole[0:block, :], pltpu.roll(whole[block : 2 * block, :], 2 * block, 1))
    ids = lane_ids(short) // block
    moved = [pltpu.roll(rows[2], 2 * block, 1), pltpu.roll(rows[3], 3 * block, 1), rows[4], pltpu.roll(rows[5], block, 1)]
    gram[block:, :] = jnp.where(ids == 0, moved[0], jnp.where(ids == 1, moved[1], jnp.where(ids == 2, moved[2], moved[3])))


def unfold_kernel(sizes, mine, other, out):
    total = (mine[...] + other[...]) / sizes.cells
    if not sizes.folded:
        out[...] = total
        return
    block = sizes.cols // 3
    top, low = total[0:block, :], total[block:, :]
    ids = lane_ids(block)
    middle = jnp.concatenate([pltpu.roll(low, 2 * block, 1), pltpu.roll(low, block, 1)], axis=0)
    second = jnp.where(ids < 2 * block, pltpu.roll(top, 2 * block, 1), middle)
    third = jnp.concatenate([low, pltpu.roll(low, 3 * block, 1)], axis=0)
    upper = jnp.concatenate([top, second, third, jnp.zeros((block, LANES), F32)], axis=0)
    across = lane_ids(LANES) // block
    down = lax.broadcasted_iota(jnp.int32, (LANES, LANES), 0) // block
    out[...] = jnp.where(down <= across, upper, upper.T)[0 : sizes.cols, 0 : sizes.cols]


def edge_kernel(sizes, ar, west_row, east_row, near, far, ends, *edges):
    n, count, lats = sizes.lons, sizes.count, sizes.lats
    last = lats - LANES
    base = count + sizes.words

    def fill(applied):
        def block(k, carry):
            start = pl.multiple_of(k * BITS, BITS)
            rows = pl.ds(start, BITS)
            ids = lane_ids(BITS)
            total = [jnp.zeros((BITS, LANES), F32) for _ in edges]
            for i in range(n + 2):
                if i >= n:
                    side = west_row if i == n else east_row
                    low, high = side[rows, 0:LANES], side[rows, last:]
                else:
                    if 0 < i < n - 1:
                        low, high = applied[i - 1, rows, 0:LANES], applied[i - 1, rows, last:]
                    else:
                        low, high = ends[min(i, 1), rows, 0:LANES], ends[min(i, 1), rows, last:]
                    low, high = low * ar[i : i + 1, 0:LANES], high * ar[i : i + 1, last:]
                moved = edge_rows_of(sizes, low, high, i)
                total = [jnp.where(ids == i, m, t) for m, t in zip(moved, total)]
            for edge, t in zip(edges, total):
                edge[rows, :] = t
            return carry

        lax.fori_loop(0, count // BITS, block, 0)

    pl.when(far_side())(lambda: fill(far))
    pl.when(jnp.logical_not(far_side()))(lambda: fill(near))
    tails = [jnp.zeros((8, LANES), F32) for _ in edges]
    ids, sub = lane_ids(8), lax.broadcasted_iota(jnp.int32, (8, LANES), 0)
    for k, row in enumerate((base, base + 2)):
        ends = [ref[row : row + 1, :] for ref in (west_row, east_row)]
        for side, end in enumerate(ends):
            moved = edge_rows_of(
                sizes,
                jnp.broadcast_to(end[:, 0:LANES], (8, LANES)),
                jnp.broadcast_to(end[:, last:], (8, LANES)),
                n + side,
            )
            spot = (ids == n + side) & (sub == k)
            tails = [jnp.where(spot, m, t) for m, t in zip(moved, tails)]
    for edge, t in zip(edges, tails):
        edge[count : count + 8, :] = t


def image_inner_kernel(part, sizes, ar, near, far, coef_near, coef_far, ends, end_coef, got_low, got_high, out):
    n, count = sizes.lons, sizes.count
    blocks = count // BITS // 2

    def fill(applied, coef):
        def block(k, carry):
            start = pl.multiple_of((part * blocks + k) * BITS, BITS)
            rows, here = pl.ds(start, BITS), pl.ds(pl.multiple_of(k * BITS, BITS), BITS)
            low_edge, high_edge = got_low[rows, :], got_high[rows, :]

            def get(i):
                source = applied[i - 1, rows, :] if 0 < i < n - 1 else ends[min(i, 1), rows, :]
                return halves(source * ar[i : i + 1, :])

            west, middle = get(0), get(1)
            for i in range(1, n - 1):
                east = get(i + 1)
                north, south = lat_shifts(
                    middle, edge_at(low_edge, i, 0), edge_at(high_edge, i, LANES - 1)
                )
                weights = rows_of(coef, (slice(i, i + 1), slice(None)))
                for h, tile in enumerate(stencil(weights, middle, east, west, north, south)):
                    out[i - 1, here, h * LANES : (h + 1) * LANES] = tile
                west, middle = middle, east
            return carry

        lax.fori_loop(0, blocks, block, 0)

    pl.when(far_side())(lambda: fill(far, coef_far))
    pl.when(jnp.logical_not(far_side()))(lambda: fill(near, coef_near))


def image_kernel(
    sizes, sk, ar, west_row, east_row, far_west, far_east, near, far, ends, end_coef,
    got_low, got_high, inner_0, inner_1, out, buffer, sems,
):
    n, count = sizes.lons, sizes.count
    base = count + sizes.words
    lat_id = lax.axis_index("lat")
    at_low = jnp.where(lat_id == 0, 0.0, 1.0)
    at_high = jnp.where(lat_id == sizes.lat_axis - 1, 0.0, 1.0)
    near_rows = [ref[base : base + 5, :] for ref in (west_row, east_row)]
    far_rows = [ref[count : count + 2, :] for ref in (far_west, far_east)]
    ghost = []
    for side in (0, 1):
        rows = near_rows[side]
        sea, east, north, kappa, area = (rows[k : k + 1] for k in range(5))
        if side == 0:
            east_w = end_coef[2, 0:1, :]
            west_w = far_rows[0][1:2] * far_rows[0][0:1] * sea
        else:
            east_w = east * sea * far_rows[1][0:1]
            west_w = end_coef[1, 1:2, :]
        lane = n + side
        low = got_low[count : count + 8, :]
        high = got_high[count : count + 8, :]
        edge_high = edge_at(high[0:1], lane, LANES - 1) * at_high
        edge_low = edge_at(low[0:1] * low[1:2], lane, 0) * at_low
        sea_parts = halves(sea)
        flow = halves(north * sea)
        sea_north, _ = lat_shifts(sea_parts, edge_low, edge_high)
        _, flow_south = lat_shifts(flow, edge_low, edge_high)
        north_w = jnp.concatenate([a * b for a, b in zip(flow, sea_north)], axis=1)
        south_w = jnp.concatenate([a * b for a, b in zip(flow_south, sea_parts)], axis=1)
        center = sea * (kappa + east_w + west_w + north_w + south_w)
        ghost.append(list(zip(*[halves(r * area) for r in (center, east_w, west_w, north_w, south_w)])))

    far_lon = far_side()

    def copy_out(k):
        start = pl.multiple_of(k * BITS, BITS)
        return pltpu.make_async_copy(buffer.at[k], out.at[pl.ds(start, BITS)], sems.at[k])

    def block_of(k, half, inner):
        start = pl.multiple_of(k * BITS, BITS)
        rows, here = pl.ds(start, BITS), pl.ds(pl.multiple_of((k - half) * BITS, BITS), BITS)
        low_edge, high_edge = got_low[rows, :], got_high[rows, :]
        for i in range(1, n - 1):
            buffer[k, :, i, :] = inner[i - 1, here, :]
        for side, i in enumerate((0, n - 1)):
            middle = halves((west_row, east_row)[side][rows, :])
            beyond = halves((far_west, far_east)[side][rows, :])
            own = halves(sk[rows, i, :])
            east, west = (own, beyond) if side == 0 else (beyond, own)
            north, south = lat_shifts(
                middle,
                edge_at(low_edge, n + side, 0),
                edge_at(high_edge, n + side, LANES - 1),
            )
            outer = stencil(ghost[side], middle, east, west, north, south)
            middle = halves(ends[side, rows, :] * ar[i : i + 1, :])
            next_in = 1 if side == 0 else n - 2
            inward = lax.select(far_lon, far[next_in - 1, rows, :], near[next_in - 1, rows, :])
            inward = halves(inward * ar[next_in : next_in + 1, :])
            east, west = (inward, outer) if side == 0 else (outer, inward)
            north, south = lat_shifts(
                middle, edge_at(low_edge, i, 0), edge_at(high_edge, i, LANES - 1)
            )
            weights = rows_of(end_coef, (slice(side, side + 1), slice(None)))
            for h, tile in enumerate(stencil(weights, middle, east, west, north, south)):
                buffer[k, :, i, h * LANES : (h + 1) * LANES] = tile
        copy_out(k).start()

    half = count // BITS // 2

    def first(k, carry):
        block_of(k, 0, inner_0)
        return carry

    def second(k, carry):
        block_of(k, half, inner_1)
        return carry

    lax.fori_loop(0, half, first, 0)
    lax.fori_loop(half, 2 * half, second, 0)
    for k in range(2 * half):
        copy_out(k).wait()


def call(kernel, sizes, outs, args, scratch=(), inputs=None, out_space=pltpu.VMEM, alias=None):
    outs = [o if isinstance(o, jax.ShapeDtypeStruct) else jax.ShapeDtypeStruct(o, F32) for o in outs]
    spaces = inputs or [pltpu.VMEM] * len(args)
    return pl.pallas_call(
        functools.partial(kernel, sizes),
        out_shape=outs,
        in_specs=[pl.BlockSpec(memory_space=space) for space in spaces],
        out_specs=[pl.BlockSpec(memory_space=out_space)] * len(outs),
        scratch_shapes=list(scratch),
        input_output_aliases=alias or {},
        compiler_params=pltpu.CompilerParams(vmem_limit_bytes=16 << 20),
    )(*args)


def exchanges():
    lons, lats = lax.axis_size("lon"), lax.axis_size("lat")
    steps = [[(i * lats + j, i * lats + (j ^ bit)) for i in range(lons) for j in range(lats)] for bit in powers(lats)]
    steps += [
        [(i * lats + j, (i ^ bit) * lats + (lats - 1 - j)) for i in range(lons) for j in range(lats)]
        for bit in powers(lons)
    ]
    return steps


def powers(limit):
    return [1 << k for k in range(limit.bit_length() - 1)]


def swap_edges(edges):
    count = lax.axis_size("lat")
    if len(edges) == 1:
        got = lax.ppermute(edges[0], "lat", [(0, 1), (1, 0)])
        return got, got
    low, high = edges
    from_low = lax.ppermute(high, "lat", [(i, (i + 1) % count) for i in range(count)])
    from_high = lax.ppermute(low, "lat", [((i + 1) % count, i) for i in range(count)])
    return from_low, from_high


def local(sketch, probe_bits, ocean, east_cond, north_cond, kappa_sq, inv_area):
    sizes = Sizes(sketch, probe_bits)
    n, lats, count = sizes.lons, sizes.lats, sizes.count
    lon_axis = lax.axis_size("lon")
    eastward = [(i, (i + 1) % lon_axis) for i in range(lon_axis)]
    westward = [((i + 1) % lon_axis, i) for i in range(lon_axis)]
    fields = (sketch, probe_bits, ocean, east_cond, north_cond, kappa_sq, inv_area)
    line, far_line = (sizes.rows, lats), (sizes.edge_rows, lats)
    edge = (sizes.edge_rows, LANES)
    edge_count = 1 if sizes.paired else 2

    shapes = [jax.ShapeDtypeStruct(f.shape, f.dtype) for f in fields]
    loaded = call(
        load_kernel,
        sizes,
        shapes + [line, line, far_line, far_line] + [edge] * edge_count,
        [pltpu.with_memory_space_constraint(f, pltpu.HBM) for f in fields],
        [pltpu.SemaphoreType.DMA((7,))],
        inputs=[pltpu.HBM] * len(fields),
    )
    fields, (to_east, to_west, far_to_east, far_to_west), packed = tuple(loaded[:7]), loaded[7:11], loaded[11:]
    sketch, probe_bits, ocean, east_cond, north_cond, kappa_sq, inv_area = fields
    west_row = lax.ppermute(to_east, "lon", eastward)
    east_row = lax.ppermute(to_west, "lon", westward)
    far_east = lax.ppermute(far_to_west, "lon", westward)
    low, high = swap_edges(packed)
    far_east = lax.ppermute(far_to_west, "lon", westward)
    far_west = lax.ppermute(far_to_east, "lon", eastward)

    def split(lons):
        return [pltpu.VMEM((sizes.cols, lons * lats), jnp.bfloat16)] * 2

    inner = [
        call(
            functools.partial(inner_kernel, far),
            sizes,
            [(n - 2, count, lats), (5, n, lats), (sizes.cols, sizes.cols)],
            fields + (low, high),
            split(n - 2) + [pltpu.VMEM((2, n + 16, lats), F32), pltpu.VMEM((n, lats), F32)],
        )
        for far in (False, True)
    ]
    (near, coef_near, partial_near), (far, coef_far, partial_far) = inner
    gram, ends, end_coef = call(
        gram_kernel,
        sizes,
        [(sizes.cols // 2, LANES) if sizes.folded else (sizes.cols, sizes.cols), (2, count, lats), (5, 2, lats)],
        (sketch, probe_bits, ocean, east_cond, kappa_sq, inv_area, west_row, east_row, low, high)
        + (coef_near, coef_far, partial_near, partial_far),
        split(2) + [pltpu.VMEM((sizes.cols, LANES), F32)],
    )
    edges = call(edge_kernel, sizes, [edge] * edge_count, (inv_area, west_row, east_row, near, far, ends))
    low2, high2 = swap_edges(edges)
    inner_images = [
        call(
            functools.partial(image_inner_kernel, part),
            sizes,
            [(n - 2, count // 2, lats)],
            (inv_area, near, far, coef_near, coef_far, ends, end_coef, low2, high2),
        )[0]
        for part in range(2)
    ]
    (image,) = call(
        image_kernel,
        sizes,
        [sketch.shape],
        (sketch, inv_area, west_row, east_row, far_west, far_east, near, far, ends, end_coef, low2, high2)
        + tuple(inner_images),
        [pltpu.VMEM((count // BITS, BITS, n, lats), F32), pltpu.SemaphoreType.DMA((count // BITS,))],
        out_space=pltpu.HBM,
    )
    steps = exchanges()
    for k, pairs in enumerate(steps):
        other = lax.ppermute(gram, ("lon", "lat"), pairs)
        if k < len(steps) - 1:
            gram = gram + other
    (gram,) = call(unfold_kernel, sizes, [(sizes.cols, sizes.cols)], (gram, other))
    return image, gram


def solution(mesh):
    field, flat = P(None, "lon", "lat"), P("lon", "lat")
    return jax.shard_map(
        local,
        mesh=mesh,
        in_specs=(field, field, flat, flat, flat, flat, flat),
        out_specs=(field, P()),
        check_vma=False,
    )
```

```python
import functools

import jax
import jax.numpy as jnp
from jax import lax
from jax.experimental import pallas as pl
from jax.experimental.pallas import tpu as pltpu
from jax.sharding import PartitionSpec as P


LANES = 128
BITS = 16
F32 = jnp.float32


def lane_ids(rows):
    return lax.broadcasted_iota(jnp.int32, (rows, LANES), 1)


def spread(words):
    shape = (BITS, words.shape[-1])
    shifts = lax.broadcasted_iota(jnp.int32, shape, 0)
    bits = jnp.bitwise_and(jnp.right_shift(jnp.broadcast_to(words, shape), shifts), 1)
    return (1 - 2 * bits).astype(F32)


def halves(field):
    return [field[:, h : h + LANES] for h in range(0, field.shape[-1], LANES)]


def lat_shifts(field, low_edge, high_edge):
    ids = lane_ids(field[0].shape[0])
    up = [pltpu.roll(part, LANES - 1, 1) for part in field] + [high_edge]
    down = [low_edge] + [pltpu.roll(part, 1, 1) for part in field]
    north = [jnp.where(ids == LANES - 1, up[h + 1], up[h]) for h in range(len(field))]
    south = [jnp.where(ids == 0, down[h], down[h + 1]) for h in range(len(field))]
    return north, south


def stencil(weights, middle, east, west, north, south):
    return [
        c * m - e * xe - w * xw - n * xn - s * xs
        for (c, e, w, n, s), m, xe, xw, xn, xs in zip(weights, middle, east, west, north, south)
    ]


def edge_at(edge, lane, target):
    return pltpu.roll(edge, (target - lane) % LANES, 1)


class Sizes:
    def __init__(self, sketch, probe_bits):
        self.count, self.lons, self.lats = sketch.shape
        self.words = probe_bits.shape[0]
        self.cols = self.count + BITS * self.words
        self.rows = -(-(self.count + self.words + 5) // 8) * 8
        self.edge_rows = -(-(self.count + 2) // 8) * 8
        self.lat_axis = lax.axis_size("lat")
        self.paired = self.lat_axis == 2
        self.folded = 4 * self.cols == 3 * LANES and self.cols % 48 == 0
        self.cells = lax.axis_size("lon") * self.lons * self.lat_axis * self.lats


def edge_rows_of(sizes, low, high, lane):
    if sizes.paired:
        first = lax.axis_index("lat") == 0
        picked = lax.select(first, high, low)
        shift = jnp.where(first, (lane + 1) % LANES, lane)
        return [pltpu.roll(picked, shift, 1)]
    return [pltpu.roll(low, lane, 1), pltpu.roll(high, (lane + 1) % LANES, 1)]


def end_row(sizes, sk, wd, oc, fields, first, r):
    count, base = sizes.count, sizes.count + sizes.words
    first[0:count, :] = sk[r]
    for w in range(sizes.words):
        first[count + w : count + w + 1, :] = wd[w, r : r + 1, :].astype(F32)
    first[base : base + 1, :] = oc[r : r + 1, :].astype(F32)
    for k, ref in enumerate(fields):
        first[base + 1 + k : base + 2 + k, :] = ref[r : r + 1, :]
    rest = first.shape[0] - base - 5
    if rest:
        first[base + 5 :, :] = jnp.zeros((rest, sizes.lats), F32)


def load_kernel(sizes, *refs):
    given, held, rows, tiles, sems = refs[:7], refs[7:14], refs[14:18], refs[18:-1], refs[-1]
    n, count = sizes.lons, sizes.count
    last = sizes.lats - LANES
    low_first = lax.axis_index("lat") == 0
    pairs = [(given[0].at[:, i, :], held[0].at[i]) for i in range(n)]
    pairs += list(zip(given[1:], held[1:]))
    copies = [pltpu.make_async_copy(g, h, sems.at[k]) for k, (g, h) in enumerate(pairs)]
    for copy in copies:
        copy.start()
    sk, wd, oc, ea, no = held[:5]
    base = sizes.words * n

    def end(ref, k):
        low, high = ref[..., 0:LANES], ref[..., last:]
        if sizes.paired:
            return lax.select(low_first, high, low)
        return (low, high)[k]

    for copy in copies[n:]:
        copy.wait()
    for k, tile in enumerate(tiles):
        words = end(wd, k).astype(F32)
        for w in range(sizes.words):
            tile[n, w * n : (w + 1) * n, :] = words[w]
        tile[n, base : base + n, :] = end(oc, k).astype(F32)
        tile[n, base + n : base + 2 * n, :] = end(no, k)
    for i in range(n):
        copies[i].wait()
        for k, tile in enumerate(tiles):
            tile[i, 0:count] = end(sk.at[i], k)
        if i in (0, n - 1):
            end_row(sizes, sk, wd, oc, held[3:], rows[0 if i else 1], i)
        if i in (1, n - 2):
            ref = rows[3 if i == 1 else 2]
            ref[0:count, :] = sk[i]
            ref[count : count + 1, :] = oc[i : i + 1, :].astype(F32)
            ref[count + 1 : count + 2, :] = ea[i : i + 1, :]
            ref[count + 2 :, :] = jnp.zeros((ref.shape[0] - count - 2, sizes.lats), F32)


def far_side():
    return lax.axis_index("lon") >= 3


def products(split_hi, split_lo):
    dims = (((1,), (1,)), ((), ()))
    main = lax.dot_general(split_hi[...], split_hi[...], dims, preferred_element_type=F32)
    cross = lax.dot_general(split_hi[...], split_lo[...], dims, preferred_element_type=F32)
    return main + cross + cross.T


def store_split(split_hi, split_lo, rows, at, scaled):
    high = scaled.astype(jnp.bfloat16)
    split_hi[rows, at] = high
    split_lo[rows, at] = (scaled - high.astype(F32)).astype(jnp.bfloat16)


def put_row(ref, where, rows, field):
    for h, part in enumerate(halves(field)):
        ref[where + (h, rows)] = part


def get_row(ref, where, i):
    tiles = [ref[where + (h, slice(i, i + 1))] for h in range(ref.shape[-3])]
    return jnp.concatenate(tiles, axis=1)


def spread_row(ref, where, i):
    tiles = [ref[where + (h, pl.ds(i, 8, stride=0))] for h in range(ref.shape[-3])]
    return [jnp.concatenate([tile] * (BITS // 8), axis=0) for tile in tiles]


def rows_of(ref, i):
    return list(zip(*[spread_row(ref, (k,), i) for k in range(5)]))


def sketch_edges(got_low, got_high, rows):
    return lambda i: (pltpu.roll(got_low[i, rows, :], 1, 1), pltpu.roll(got_high[i, rows, :], LANES - 1, 1))


def probe_edges(sizes, w, got_low, got_high):
    n = sizes.lons

    def edges(i):
        at = w * n + i
        low, high = (got[n, at : at + 1, :].astype(jnp.int32) for got in (got_low, got_high))
        return spread(pltpu.roll(low, 1, 1)), spread(pltpu.roll(high, LANES - 1, 1))

    return edges


def inner_kernel(
    far, sizes, sk, wd, oc, ea, no, ka, ar, got_low, got_high,
    applied, coef, partial, split_hi, split_lo, ext, root,
):
    n, count, lats, words = sizes.lons, sizes.count, sizes.lats, sizes.words

    @pl.when(far_side() == far)
    def _():
        lat_id = lax.axis_index("lat")
        sea = oc[...].astype(F32)
        ext[0, 8 : 8 + n, :] = sea
        ext[0, 8 + n : 9 + n, :] = jnp.zeros((1, lats), F32)
        ext[1, 8 : 8 + n, :] = ea[...] * sea * ext[0, 9 : 9 + n, :]
        ext[1, 7:8, :] = jnp.zeros((1, lats), F32)
        east_w = ext[1, 8 : 8 + n, :]
        west_w = ext[1, 7 : 7 + n, :]

        sea_parts = halves(sea)
        half_north = [no[:, h * LANES : (h + 1) * LANES] * part for h, part in enumerate(sea_parts)]
        at_low = jnp.where(lat_id == 0, 0.0, 1.0)
        at_high = jnp.where(lat_id == sizes.lat_axis - 1, 0.0, 1.0)
        edge_high = pltpu.roll(got_high[n, words * n : (words + 1) * n, :], LANES - 1, 1) * at_high
        flow_low = got_low[n, words * n : (words + 1) * n, :] * got_low[n, (words + 1) * n : (words + 2) * n, :]
        edge_low = pltpu.roll(flow_low, 1, 1) * at_low
        sea_north, _ = lat_shifts(sea_parts, edge_low, edge_high)
        _, flow_south = lat_shifts(half_north, edge_low, edge_high)
        north_w = jnp.concatenate([a * b for a, b in zip(half_north, sea_north)], axis=1)
        south_w = jnp.concatenate([a * b for a, b in zip(flow_south, sea_parts)], axis=1)
        put_row(coef, (0,), slice(0, n), sea * (ka[...] + east_w + west_w + north_w + south_w))
        put_row(coef, (1,), slice(0, n), east_w)
        put_row(coef, (2,), slice(0, n), west_w)
        put_row(coef, (3,), slice(0, n), north_w)
        put_row(coef, (4,), slice(0, n), south_w)
        put_row(coef, (5,), slice(0, n), ar[...])
        put_row(root, (), slice(0, n), jnp.sqrt(ar[...]))

        def one_block(start, get, edges, keep):
            rows = pl.ds(start, BITS)
            west, middle = get(0), get(1)
            for i in range(1, n - 1):
                east = get(i + 1)
                north, south = lat_shifts(middle, *edges(i))
                weights, scale = rows_of(coef, i), spread_row(root, (), i)
                for h, part in enumerate(stencil(weights, middle, east, west, north, south)):
                    here = slice(h * LANES, (h + 1) * LANES)
                    if keep:
                        applied[i - 1, rows, here] = part
                    at = slice((i - 1) * lats + h * LANES, (i - 1) * lats + (h + 1) * LANES)
                    store_split(split_hi, split_lo, rows, at, part * scale[h])
                west, middle = middle, east

        def sketch_block(k, carry):
            start = pl.multiple_of(k * BITS, BITS)
            rows = pl.ds(start, BITS)
            one_block(start, lambda i: halves(sk[i, rows, :]), sketch_edges(got_low, got_high, rows), True)
            return carry

        lax.fori_loop(0, count // BITS, sketch_block, 0)
        for w in range(words):
            one_block(
                count + w * BITS,
                lambda i: [spread(part) for part in halves(wd[w, i : i + 1, :])],
                probe_edges(sizes, w, got_low, got_high),
                False,
            )
        partial[...] = products(split_hi, split_lo)


def gram_kernel(
    sizes, sk, wd, oc, ea, ka, ar, west_row, east_row, got_low, got_high,
    coef_near, coef_far, partial_near, partial_far,
    gram, ends, end_coef, split_hi, split_lo, whole,
):
    n, count, lats, words = sizes.lons, sizes.count, sizes.lats, sizes.words
    base = count + words
    far = far_side()

    def inner(k, i):
        return lax.select(far, get_row(coef_far, (k,), i), get_row(coef_near, (k,), i))

    root = []
    for side, i in enumerate((0, n - 1)):
        sea = oc[i : i + 1, :].astype(F32)
        east_w, west_w, north_w, south_w = (inner(k, i) for k in range(1, 5))
        if side == 0:
            west_w = west_row[base + 1 : base + 2, :] * west_row[base : base + 1, :] * sea
        else:
            east_w = ea[i : i + 1, :] * sea * east_row[base : base + 1, :]
        center = sea * (ka[i : i + 1, :] + east_w + west_w + north_w + south_w)
        for k, row in enumerate((center, east_w, west_w, north_w, south_w)):
            put_row(end_coef, (k,), slice(side, side + 1), row)
        root.append(jnp.sqrt(ar[i : i + 1, :]))

    def one_block(start, get, edges, keep):
        rows = pl.ds(start, BITS)
        for side, i in enumerate((0, n - 1)):
            middle = get(i)
            north, south = lat_shifts(middle, *edges(i))
            weights = rows_of(end_coef, side)
            for h, part in enumerate(stencil(weights, middle, get(i + 1), get(i - 1), north, south)):
                here = slice(h * LANES, (h + 1) * LANES)
                if keep:
                    ends[side, rows, here] = part
                at = slice(side * lats + h * LANES, side * lats + (h + 1) * LANES)
                store_split(split_hi, split_lo, rows, at, part * root[side][:, here])

    for start in range(0, count, BITS):
        rows = slice(start, start + BITS)

        def get(i):
            if i == -1:
                return halves(west_row[rows, :])
            if i == n:
                return halves(east_row[rows, :])
            return halves(sk[i, rows, :])

        one_block(start, get, sketch_edges(got_low, got_high, rows), True)
    for w in range(words):

        def get(i):
            if i == -1:
                row = west_row[count + w : count + w + 1, :].astype(jnp.int32)
            elif i == n:
                row = east_row[count + w : count + w + 1, :].astype(jnp.int32)
            else:
                row = wd[w, i : i + 1, :]
            return [spread(part) for part in halves(row)]

        one_block(count + w * BITS, get, probe_edges(sizes, w, got_low, got_high), False)

    total = lax.select(far, partial_far[...], partial_near[...]) + products(split_hi, split_lo)
    if not sizes.folded:
        gram[...] = total
        return
    block, short = sizes.cols // 3, sizes.cols // 6
    whole[:, 0 : sizes.cols] = total
    rows = [whole[k * short : (k + 1) * short, :] for k in range(6)]
    ids = lane_ids(block)
    gram[0:block, :] = jnp.where(ids < sizes.cols, whole[0:block, :], pltpu.roll(whole[block : 2 * block, :], 2 * block, 1))
    ids = lane_ids(short) // block
    moved = [pltpu.roll(rows[2], 2 * block, 1), pltpu.roll(rows[3], 3 * block, 1), rows[4], pltpu.roll(rows[5], block, 1)]
    gram[block:, :] = jnp.where(ids == 0, moved[0], jnp.where(ids == 1, moved[1], jnp.where(ids == 2, moved[2], moved[3])))


def unfold_kernel(sizes, mine, other, out):
    total = (mine[...] + other[...]) / sizes.cells
    if not sizes.folded:
        out[...] = total
        return
    block = sizes.cols // 3
    top, low = total[0:block, :], total[block:, :]
    ids = lane_ids(block)
    middle = jnp.concatenate([pltpu.roll(low, 2 * block, 1), pltpu.roll(low, block, 1)], axis=0)
    second = jnp.where(ids < 2 * block, pltpu.roll(top, 2 * block, 1), middle)
    third = jnp.concatenate([low, pltpu.roll(low, 3 * block, 1)], axis=0)
    upper = jnp.concatenate([top, second, third, jnp.zeros((block, LANES), F32)], axis=0)
    across = lane_ids(LANES) // block
    down = lax.broadcasted_iota(jnp.int32, (LANES, LANES), 0) // block
    out[...] = jnp.where(down <= across, upper, upper.T)[0 : sizes.cols, 0 : sizes.cols]


def edge_kernel(sizes, ar, west_row, east_row, near, far, ends, *edges):
    n, count, lats = sizes.lons, sizes.count, sizes.lats
    last = lats - LANES
    base = count + sizes.words

    def fill(applied):
        def block(k, carry):
            start = pl.multiple_of(k * BITS, BITS)
            rows = pl.ds(start, BITS)
            ids = lane_ids(BITS)
            total = [jnp.zeros((BITS, LANES), F32) for _ in edges]
            for i in range(n + 2):
                if i >= n:
                    side = west_row if i == n else east_row
                    low, high = side[rows, 0:LANES], side[rows, last:]
                else:
                    if 0 < i < n - 1:
                        low, high = applied[i - 1, rows, 0:LANES], applied[i - 1, rows, last:]
                    else:
                        low, high = ends[min(i, 1), rows, 0:LANES], ends[min(i, 1), rows, last:]
                    low, high = low * ar[i : i + 1, 0:LANES], high * ar[i : i + 1, last:]
                moved = edge_rows_of(sizes, low, high, i)
                total = [jnp.where(ids == i, m, t) for m, t in zip(moved, total)]
            for edge, t in zip(edges, total):
                edge[rows, :] = t
            return carry

        lax.fori_loop(0, count // BITS, block, 0)

    pl.when(far_side())(lambda: fill(far))
    pl.when(jnp.logical_not(far_side()))(lambda: fill(near))
    tails = [jnp.zeros((8, LANES), F32) for _ in edges]
    ids, sub = lane_ids(8), lax.broadcasted_iota(jnp.int32, (8, LANES), 0)
    for k, row in enumerate((base, base + 2)):
        ends = [ref[row : row + 1, :] for ref in (west_row, east_row)]
        for side, end in enumerate(ends):
            moved = edge_rows_of(
                sizes,
                jnp.broadcast_to(end[:, 0:LANES], (8, LANES)),
                jnp.broadcast_to(end[:, last:], (8, LANES)),
                n + side,
            )
            spot = (ids == n + side) & (sub == k)
            tails = [jnp.where(spot, m, t) for m, t in zip(moved, tails)]
    for edge, t in zip(edges, tails):
        edge[count : count + 8, :] = t


def image_inner_kernel(part, sizes, near, far, coef_near, coef_far, ends, got_low, got_high, out):
    n, count = sizes.lons, sizes.count
    blocks = count // BITS // 2

    def fill(applied, coef):
        def block(k, carry):
            start = pl.multiple_of((part * blocks + k) * BITS, BITS)
            rows, here = pl.ds(start, BITS), pl.ds(pl.multiple_of(k * BITS, BITS), BITS)
            low_edge, high_edge = got_low[rows, :], got_high[rows, :]

            def get(i):
                source = applied[i - 1, rows, :] if 0 < i < n - 1 else ends[min(i, 1), rows, :]
                return [a * b for a, b in zip(halves(source), spread_row(coef, (5,), i))]

            west, middle = get(0), get(1)
            for i in range(1, n - 1):
                east = get(i + 1)
                north, south = lat_shifts(
                    middle, edge_at(low_edge, i, 0), edge_at(high_edge, i, LANES - 1)
                )
                weights = rows_of(coef, i)
                for h, tile in enumerate(stencil(weights, middle, east, west, north, south)):
                    out[i - 1, here, h * LANES : (h + 1) * LANES] = tile
                west, middle = middle, east
            return carry

        lax.fori_loop(0, blocks, block, 0)

    pl.when(far_side())(lambda: fill(far, coef_far))
    pl.when(jnp.logical_not(far_side()))(lambda: fill(near, coef_near))


def image_kernel(
    sizes, sk, ar, west_row, east_row, far_west, far_east, near, far, ends, end_coef,
    got_low, got_high, inner_0, inner_1, out, buffer, sems,
):
    n, count = sizes.lons, sizes.count
    base = count + sizes.words
    lat_id = lax.axis_index("lat")
    at_low = jnp.where(lat_id == 0, 0.0, 1.0)
    at_high = jnp.where(lat_id == sizes.lat_axis - 1, 0.0, 1.0)
    near_rows = [ref[base : base + 5, :] for ref in (west_row, east_row)]
    far_rows = [ref[count : count + 2, :] for ref in (far_west, far_east)]
    ghost = []
    for side in (0, 1):
        rows = near_rows[side]
        sea, east, north, kappa, area = (rows[k : k + 1] for k in range(5))
        if side == 0:
            east_w = get_row(end_coef, (2,), 0)
            west_w = far_rows[0][1:2] * far_rows[0][0:1] * sea
        else:
            east_w = east * sea * far_rows[1][0:1]
            west_w = get_row(end_coef, (1,), 1)
        lane = n + side
        low = got_low[count : count + 8, :]
        high = got_high[count : count + 8, :]
        edge_high = edge_at(high[0:1], lane, LANES - 1) * at_high
        edge_low = edge_at(low[0:1] * low[1:2], lane, 0) * at_low
        sea_parts = halves(sea)
        flow = halves(north * sea)
        sea_north, _ = lat_shifts(sea_parts, edge_low, edge_high)
        _, flow_south = lat_shifts(flow, edge_low, edge_high)
        north_w = jnp.concatenate([a * b for a, b in zip(flow, sea_north)], axis=1)
        south_w = jnp.concatenate([a * b for a, b in zip(flow_south, sea_parts)], axis=1)
        center = sea * (kappa + east_w + west_w + north_w + south_w)
        ghost.append(list(zip(*[halves(r * area) for r in (center, east_w, west_w, north_w, south_w)])))

    far_lon = far_side()
    copies = []
    for part, inner in enumerate((inner_0, inner_1)):
        columns = pl.ds(part * (count // 2), count // 2)
        copies += [(inner.at[i - 1], out.at[columns, i, :]) for i in range(1, n - 1)]
    copies += [(buffer.at[side], out.at[:, i, :]) for side, i in enumerate((0, n - 1))]
    copies = [pltpu.make_async_copy(a, b, sems.at[k]) for k, (a, b) in enumerate(copies)]
    for copy in copies[:-2]:
        copy.start()

    def block(k, carry):
        start = pl.multiple_of(k * BITS, BITS)
        rows = pl.ds(start, BITS)
        low_edge, high_edge = got_low[rows, :], got_high[rows, :]
        for side, i in enumerate((0, n - 1)):
            middle = halves((west_row, east_row)[side][rows, :])
            beyond = halves((far_west, far_east)[side][rows, :])
            own = halves(sk[i, rows, :])
            east, west = (own, beyond) if side == 0 else (beyond, own)
            north, south = lat_shifts(
                middle,
                edge_at(low_edge, n + side, 0),
                edge_at(high_edge, n + side, LANES - 1),
            )
            outer = stencil(ghost[side], middle, east, west, north, south)
            middle = halves(ends[side, rows, :] * ar[i : i + 1, :])
            next_in = 1 if side == 0 else n - 2
            inward = lax.select(far_lon, far[next_in - 1, rows, :], near[next_in - 1, rows, :])
            inward = halves(inward * ar[next_in : next_in + 1, :])
            east, west = (inward, outer) if side == 0 else (outer, inward)
            north, south = lat_shifts(
                middle, edge_at(low_edge, i, 0), edge_at(high_edge, i, LANES - 1)
            )
            weights = rows_of(end_coef, side)
            for h, tile in enumerate(stencil(weights, middle, east, west, north, south)):
                buffer[side, rows, h * LANES : (h + 1) * LANES] = tile
        return carry

    lax.fori_loop(0, count // BITS, block, 0)
    for copy in copies[-2:]:
        copy.start()
    for copy in copies:
        copy.wait()


def call(kernel, sizes, outs, args, scratch=(), inputs=None, out_space=pltpu.VMEM, alias=None):
    outs = [o if isinstance(o, jax.ShapeDtypeStruct) else jax.ShapeDtypeStruct(o, F32) for o in outs]
    spaces = inputs or [pltpu.VMEM] * len(args)
    return pl.pallas_call(
        functools.partial(kernel, sizes),
        out_shape=outs,
        in_specs=[pl.BlockSpec(memory_space=space) for space in spaces],
        out_specs=[pl.BlockSpec(memory_space=out_space)] * len(outs),
        scratch_shapes=list(scratch),
        input_output_aliases=alias or {},
        compiler_params=pltpu.CompilerParams(vmem_limit_bytes=16 << 20),
    )(*args)


def exchanges():
    lons, lats = lax.axis_size("lon"), lax.axis_size("lat")
    steps = [[(i * lats + j, i * lats + (j ^ bit)) for i in range(lons) for j in range(lats)] for bit in powers(lats)]
    lon_bits = powers(lons)
    lon_bits[:2] = reversed(lon_bits[:2])
    steps += [
        [(i * lats + j, (i ^ bit) * lats + (lats - 1 - j)) for i in range(lons) for j in range(lats)]
        for bit in lon_bits
    ]
    return steps


def powers(limit):
    return [1 << k for k in range(limit.bit_length() - 1)]


def swap_edges(edges):
    count = lax.axis_size("lat")
    if len(edges) == 1:
        got = lax.ppermute(edges[0], "lat", [(0, 1), (1, 0)])
        return got, got
    low, high = edges
    from_low = lax.ppermute(high, "lat", [(i, (i + 1) % count) for i in range(count)])
    from_high = lax.ppermute(low, "lat", [((i + 1) % count, i) for i in range(count)])
    return from_low, from_high


def local(sketch, probe_bits, ocean, east_cond, north_cond, kappa_sq, inv_area):
    sizes = Sizes(sketch, probe_bits)
    n, lats, count = sizes.lons, sizes.lats, sizes.count
    lon_axis = lax.axis_size("lon")
    eastward = [(i, (i + 1) % lon_axis) for i in range(lon_axis)]
    westward = [((i + 1) % lon_axis, i) for i in range(lon_axis)]
    fields = (sketch, probe_bits, ocean, east_cond, north_cond, kappa_sq, inv_area)
    line, far_line = (sizes.rows, lats), (sizes.edge_rows, lats)
    edge = (sizes.edge_rows, LANES)
    edge_count = 1 if sizes.paired else 2

    shapes = [jax.ShapeDtypeStruct(f.shape, f.dtype) for f in fields]
    shapes[0] = jax.ShapeDtypeStruct((n, count, lats), F32)
    loaded = call(
        load_kernel,
        sizes,
        shapes + [line, line, far_line, far_line] + [(n + 1, max(count, (sizes.words + 2) * n), LANES)] * edge_count,
        [pltpu.with_memory_space_constraint(f, pltpu.HBM) for f in fields],
        [pltpu.SemaphoreType.DMA((6 + n,))],
        inputs=[pltpu.HBM] * len(fields),
    )
    fields, (to_east, to_west, far_to_east, far_to_west), packed = tuple(loaded[:7]), loaded[7:11], loaded[11:]
    sketch, probe_bits, ocean, east_cond, north_cond, kappa_sq, inv_area = fields
    west_row = lax.ppermute(to_east, "lon", eastward)
    east_row = lax.ppermute(to_west, "lon", westward)
    far_east = lax.ppermute(far_to_west, "lon", westward)
    low, high = swap_edges(packed)
    far_east = lax.ppermute(far_to_west, "lon", westward)
    far_west = lax.ppermute(far_to_east, "lon", eastward)

    def split(lons):
        return [pltpu.VMEM((sizes.cols, lons * lats), jnp.bfloat16)] * 2

    inner = [
        call(
            functools.partial(inner_kernel, far),
            sizes,
            [(n - 2, count, lats), (6, lats // LANES, n + 8, LANES), (sizes.cols, sizes.cols)],
            fields + (low, high),
            split(n - 2) + [pltpu.VMEM((2, n + 16, lats), F32), pltpu.VMEM((lats // LANES, n + 8, LANES), F32)],
        )
        for far in (False, True)
    ]
    (near, coef_near, partial_near), (far, coef_far, partial_far) = inner
    gram, ends, end_coef = call(
        gram_kernel,
        sizes,
        [(sizes.cols // 2, LANES) if sizes.folded else (sizes.cols, sizes.cols), (2, count, lats), (5, lats // LANES, 16, LANES)],
        (sketch, probe_bits, ocean, east_cond, kappa_sq, inv_area, west_row, east_row, low, high)
        + (coef_near, coef_far, partial_near, partial_far),
        split(2) + [pltpu.VMEM((sizes.cols, LANES), F32)],
    )
    edges = call(edge_kernel, sizes, [edge] * edge_count, (inv_area, west_row, east_row, near, far, ends))
    low2, high2 = swap_edges(edges)
    inner_images = [
        call(
            functools.partial(image_inner_kernel, part),
            sizes,
            [(n - 2, count // 2, lats)],
            (near, far, coef_near, coef_far, ends, low2, high2),
        )[0]
        for part in range(2)
    ]
    (image,) = call(
        image_kernel,
        sizes,
        [(count, n, lats)],
        (sketch, inv_area, west_row, east_row, far_west, far_east, near, far, ends, end_coef, low2, high2)
        + tuple(inner_images),
        [pltpu.VMEM((2, count, lats), F32), pltpu.SemaphoreType.DMA((2 * n - 2,))],
        out_space=pltpu.HBM,
    )
    steps = exchanges()
    for k, pairs in enumerate(steps):
        other = lax.ppermute(gram, ("lon", "lat"), pairs)
        if k < len(steps) - 1:
            gram = gram + other
    (gram,) = call(unfold_kernel, sizes, [(sizes.cols, sizes.cols)], (gram, other))
    return image, gram


def solution(mesh):
    field, flat = P(None, "lon", "lat"), P("lon", "lat")
    return jax.shard_map(
        local,
        mesh=mesh,
        in_specs=(field, field, flat, flat, flat, flat, flat),
        out_specs=(field, P()),
        check_vma=False,
    )
```

```python
import functools

import jax
import jax.numpy as jnp
from jax import lax
from jax.experimental import pallas as pl
from jax.experimental.pallas import tpu as pltpu
from jax.sharding import PartitionSpec as P


LANES = 128
BITS = 16
FOLDS = ((8,), (7,), (6,), (5,), (9, 10, 11))
F32 = jnp.float32


def lane_ids(rows):
    return lax.broadcasted_iota(jnp.int32, (rows, LANES), 1)


def spread(words):
    shape = (BITS, words.shape[-1])
    shifts = lax.broadcasted_iota(jnp.int32, shape, 0)
    bits = jnp.bitwise_and(jnp.right_shift(jnp.broadcast_to(words, shape), shifts), 1)
    return (1 - 2 * bits).astype(F32)


def halves(field):
    return [field[:, h : h + LANES] for h in range(0, field.shape[-1], LANES)]


def lat_shifts(field, low_edge, high_edge):
    ids = lane_ids(field[0].shape[0])
    up = [pltpu.roll(part, LANES - 1, 1) for part in field] + [high_edge]
    down = [low_edge] + [pltpu.roll(part, 1, 1) for part in field]
    north = [jnp.where(ids == LANES - 1, up[h + 1], up[h]) for h in range(len(field))]
    south = [jnp.where(ids == 0, down[h], down[h + 1]) for h in range(len(field))]
    return north, south


def stencil(weights, middle, east, west, north, south):
    return [
        c * m - e * xe - w * xw - n * xn - s * xs
        for (c, e, w, n, s), m, xe, xw, xn, xs in zip(weights, middle, east, west, north, south)
    ]


def edge_at(edge, lane, target):
    return pltpu.roll(edge, (target - lane) % LANES, 1)


def fold_place(sizes, r, other):
    start = sizes.cols
    for before in FOLDS[r]:
        width = sizes.cols - 8 * before
        if before == other:
            return start % LANES, width
        start += width


class Sizes:
    def __init__(self, sketch, probe_bits):
        self.count, self.lons, self.lats = sketch.shape
        self.words = probe_bits.shape[0]
        self.cols = self.count + BITS * self.words
        self.rows = -(-(self.count + self.words + 5) // 8) * 8
        self.edge_rows = -(-(self.count + 2) // 8) * 8
        self.lat_axis = lax.axis_size("lat")
        self.paired = self.lat_axis == 2
        self.folded = 4 * self.cols == 3 * LANES
        self.cells = lax.axis_size("lon") * self.lons * self.lat_axis * self.lats


def edge_rows_of(sizes, low, high, lane):
    if sizes.paired:
        first = lax.axis_index("lat") == 0
        picked = lax.select(first, high, low)
        shift = jnp.where(first, (lane + 1) % LANES, lane)
        return [pltpu.roll(picked, shift, 1)]
    return [pltpu.roll(low, lane, 1), pltpu.roll(high, (lane + 1) % LANES, 1)]


def end_row(sizes, sk, wd, oc, fields, first, r):
    count, base = sizes.count, sizes.count + sizes.words
    first[0:count, :] = sk[r]
    for w in range(sizes.words):
        first[count + w : count + w + 1, :] = wd[w, r : r + 1, :].astype(F32)
    first[base : base + 1, :] = oc[r : r + 1, :].astype(F32)
    for k, ref in enumerate(fields):
        first[base + 1 + k : base + 2 + k, :] = ref[r : r + 1, :]
    rest = first.shape[0] - base - 5
    if rest:
        first[base + 5 :, :] = jnp.zeros((rest, sizes.lats), F32)


def load_kernel(sizes, *refs):
    given, held, rows, tiles, sems = refs[:7], refs[7:14], refs[14:18], refs[18:-1], refs[-1]
    n, count = sizes.lons, sizes.count
    last = sizes.lats - LANES
    low_first = lax.axis_index("lat") == 0
    pairs = [(given[0].at[:, i, :], held[0].at[i]) for i in range(n)]
    pairs += list(zip(given[1:], held[1:]))
    copies = [pltpu.make_async_copy(g, h, sems.at[k]) for k, (g, h) in enumerate(pairs)]
    for copy in copies:
        copy.start()
    sk, wd, oc, ea, no = held[:5]
    base = sizes.words * n

    def end(ref, k):
        low, high = ref[..., 0:LANES], ref[..., last:]
        if sizes.paired:
            return lax.select(low_first, high, low)
        return (low, high)[k]

    for copy in copies[n:]:
        copy.wait()
    for k, tile in enumerate(tiles):
        words = end(wd, k).astype(F32)
        for w in range(sizes.words):
            tile[n, w * n : (w + 1) * n, :] = words[w]
        tile[n, base : base + n, :] = end(oc, k).astype(F32)
        tile[n, base + n : base + 2 * n, :] = end(no, k)
    for i in range(n):
        copies[i].wait()
        for k, tile in enumerate(tiles):
            tile[i, 0:count] = end(sk.at[i], k)
        if i in (0, n - 1):
            end_row(sizes, sk, wd, oc, held[3:], rows[0 if i else 1], i)
        if i in (1, n - 2):
            ref = rows[3 if i == 1 else 2]
            ref[0:count, :] = sk[i]
            ref[count : count + 1, :] = oc[i : i + 1, :].astype(F32)
            ref[count + 1 : count + 2, :] = ea[i : i + 1, :]
            ref[count + 2 :, :] = jnp.zeros((ref.shape[0] - count - 2, sizes.lats), F32)


def far_side():
    return lax.axis_index("lon") >= 5


def products(split_hi, split_lo):
    dims = (((1,), (1,)), ((), ()))
    main = lax.dot_general(split_hi[...], split_hi[...], dims, preferred_element_type=F32)
    cross = lax.dot_general(split_hi[...], split_lo[...], dims, preferred_element_type=F32)
    return main + cross + cross.T


def store_split(split_hi, split_lo, rows, at, scaled):
    high = scaled.astype(jnp.bfloat16)
    split_hi[rows, at] = high
    split_lo[rows, at] = (scaled - high.astype(F32)).astype(jnp.bfloat16)


def put_row(ref, where, rows, field):
    for h, part in enumerate(halves(field)):
        ref[where + (h, rows)] = part


def get_row(ref, where, i):
    tiles = [ref[where + (h, slice(i, i + 1))] for h in range(ref.shape[-3])]
    return jnp.concatenate(tiles, axis=1)


def spread_row(ref, where, i):
    tiles = [ref[where + (h, pl.ds(i, 8, stride=0))] for h in range(ref.shape[-3])]
    return [jnp.concatenate([tile] * (BITS // 8), axis=0) for tile in tiles]


def rows_of(ref, i):
    return list(zip(*[spread_row(ref, (k,), i) for k in range(5)]))


def sketch_edges(got_low, got_high, rows):
    return lambda i: (pltpu.roll(got_low[i, rows, :], 1, 1), pltpu.roll(got_high[i, rows, :], LANES - 1, 1))


def probe_edges(sizes, w, got_low, got_high):
    n = sizes.lons

    def edges(i):
        at = w * n + i
        low, high = (got[n, at : at + 1, :].astype(jnp.int32) for got in (got_low, got_high))
        return spread(pltpu.roll(low, 1, 1)), spread(pltpu.roll(high, LANES - 1, 1))

    return edges


def inner_kernel(
    far, sizes, sk, wd, oc, ea, no, ka, ar, got_low, got_high,
    applied, coef, partial, split_hi, split_lo, ext, root,
):
    n, count, lats, words = sizes.lons, sizes.count, sizes.lats, sizes.words

    @pl.when(far_side() == far)
    def _():
        lat_id = lax.axis_index("lat")
        sea = oc[...].astype(F32)
        ext[0, 8 : 8 + n, :] = sea
        ext[0, 8 + n : 9 + n, :] = jnp.zeros((1, lats), F32)
        ext[1, 8 : 8 + n, :] = ea[...] * sea * ext[0, 9 : 9 + n, :]
        ext[1, 7:8, :] = jnp.zeros((1, lats), F32)
        east_w = ext[1, 8 : 8 + n, :]
        west_w = ext[1, 7 : 7 + n, :]

        sea_parts = halves(sea)
        half_north = [no[:, h * LANES : (h + 1) * LANES] * part for h, part in enumerate(sea_parts)]
        at_low = jnp.where(lat_id == 0, 0.0, 1.0)
        at_high = jnp.where(lat_id == sizes.lat_axis - 1, 0.0, 1.0)
        edge_high = pltpu.roll(got_high[n, words * n : (words + 1) * n, :], LANES - 1, 1) * at_high
        flow_low = got_low[n, words * n : (words + 1) * n, :] * got_low[n, (words + 1) * n : (words + 2) * n, :]
        edge_low = pltpu.roll(flow_low, 1, 1) * at_low
        sea_north, _ = lat_shifts(sea_parts, edge_low, edge_high)
        _, flow_south = lat_shifts(half_north, edge_low, edge_high)
        north_w = jnp.concatenate([a * b for a, b in zip(half_north, sea_north)], axis=1)
        south_w = jnp.concatenate([a * b for a, b in zip(flow_south, sea_parts)], axis=1)
        put_row(coef, (0,), slice(0, n), sea * (ka[...] + east_w + west_w + north_w + south_w))
        put_row(coef, (1,), slice(0, n), east_w)
        put_row(coef, (2,), slice(0, n), west_w)
        put_row(coef, (3,), slice(0, n), north_w)
        put_row(coef, (4,), slice(0, n), south_w)
        put_row(coef, (5,), slice(0, n), ar[...])
        put_row(root, (), slice(0, n), jnp.sqrt(ar[...]))

        def one_block(start, get, edges, keep):
            rows = pl.ds(start, BITS)
            west, middle = get(0), get(1)
            for i in range(1, n - 1):
                east = get(i + 1)
                north, south = lat_shifts(middle, *edges(i))
                weights, scale = rows_of(coef, i), spread_row(root, (), i)
                for h, part in enumerate(stencil(weights, middle, east, west, north, south)):
                    here = slice(h * LANES, (h + 1) * LANES)
                    if keep:
                        applied[i - 1, rows, here] = part
                    at = slice((i - 1) * lats + h * LANES, (i - 1) * lats + (h + 1) * LANES)
                    store_split(split_hi, split_lo, rows, at, part * scale[h])
                west, middle = middle, east

        def sketch_block(k, carry):
            start = pl.multiple_of(k * BITS, BITS)
            rows = pl.ds(start, BITS)
            one_block(start, lambda i: halves(sk[i, rows, :]), sketch_edges(got_low, got_high, rows), True)
            return carry

        lax.fori_loop(0, count // BITS, sketch_block, 0)
        for w in range(words):
            one_block(
                count + w * BITS,
                lambda i: [spread(part) for part in halves(wd[w, i : i + 1, :])],
                probe_edges(sizes, w, got_low, got_high),
                False,
            )
        partial[...] = products(split_hi, split_lo)


def gram_kernel(
    sizes, sk, wd, oc, ea, ka, ar, west_row, east_row, got_low, got_high,
    coef_near, coef_far, partial_near, partial_far,
    gram, ends, end_coef, split_hi, split_lo, whole,
):
    n, count, lats, words = sizes.lons, sizes.count, sizes.lats, sizes.words
    base = count + words
    far = far_side()

    def inner(k, i):
        return lax.select(far, get_row(coef_far, (k,), i), get_row(coef_near, (k,), i))

    root = []
    for side, i in enumerate((0, n - 1)):
        sea = oc[i : i + 1, :].astype(F32)
        east_w, west_w, north_w, south_w = (inner(k, i) for k in range(1, 5))
        if side == 0:
            west_w = west_row[base + 1 : base + 2, :] * west_row[base : base + 1, :] * sea
        else:
            east_w = ea[i : i + 1, :] * sea * east_row[base : base + 1, :]
        center = sea * (ka[i : i + 1, :] + east_w + west_w + north_w + south_w)
        for k, row in enumerate((center, east_w, west_w, north_w, south_w)):
            put_row(end_coef, (k,), slice(side, side + 1), row)
        root.append(jnp.sqrt(ar[i : i + 1, :]))

    def one_block(start, get, edges, keep):
        rows = pl.ds(start, BITS)
        for side, i in enumerate((0, n - 1)):
            middle = get(i)
            north, south = lat_shifts(middle, *edges(i))
            weights = rows_of(end_coef, side)
            for h, part in enumerate(stencil(weights, middle, get(i + 1), get(i - 1), north, south)):
                here = slice(h * LANES, (h + 1) * LANES)
                if keep:
                    ends[side, rows, here] = part
                at = slice(side * lats + h * LANES, side * lats + (h + 1) * LANES)
                store_split(split_hi, split_lo, rows, at, part * root[side][:, here])

    for start in range(0, count, BITS):
        rows = slice(start, start + BITS)

        def get(i):
            if i == -1:
                return halves(west_row[rows, :])
            if i == n:
                return halves(east_row[rows, :])
            return halves(sk[i, rows, :])

        one_block(start, get, sketch_edges(got_low, got_high, rows), True)
    for w in range(words):

        def get(i):
            if i == -1:
                row = west_row[count + w : count + w + 1, :].astype(jnp.int32)
            elif i == n:
                row = east_row[count + w : count + w + 1, :].astype(jnp.int32)
            else:
                row = wd[w, i : i + 1, :]
            return [spread(part) for part in halves(row)]

        one_block(count + w * BITS, get, probe_edges(sizes, w, got_low, got_high), False)

    total = lax.select(far, partial_far[...], partial_near[...]) + products(split_hi, split_lo)
    if not sizes.folded:
        gram[...] = total
        return
    whole[:, 0 : sizes.cols] = total
    ids = lane_ids(8)
    for r, parts in enumerate(FOLDS):
        kept = whole[8 * r : 8 * r + 8, :]
        for other in parts:
            start, width = fold_place(sizes, r, other)
            moved = pltpu.roll(whole[8 * other : 8 * other + 8, :], (start - 8 * other) % LANES, 1)
            kept = jnp.where((ids - start) % LANES < width, moved, kept)
        gram[8 * r : 8 * r + 8, :] = kept


def unfold_kernel(sizes, mine, other, out):
    total = (mine[...] + other[...]) / sizes.cells
    if not sizes.folded:
        out[...] = total
        return
    blocks = {}
    for r, parts in enumerate(FOLDS):
        kept = total[8 * r : 8 * r + 8, :]
        blocks[r] = kept
        for other in parts:
            start, _ = fold_place(sizes, r, other)
            blocks[other] = pltpu.roll(kept, (8 * other - start) % LANES, 1)
    rows = [blocks[r] for r in sorted(blocks)]
    upper = jnp.concatenate(rows + [jnp.zeros((LANES - sizes.cols, LANES), F32)], axis=0)
    across = lane_ids(LANES) // 8
    down = lax.broadcasted_iota(jnp.int32, (LANES, LANES), 0) // 8
    out[...] = jnp.where(down <= across, upper, upper.T)[0 : sizes.cols, 0 : sizes.cols]


def edge_kernel(sizes, ar, west_row, east_row, near, far, ends, *edges):
    n, count, lats = sizes.lons, sizes.count, sizes.lats
    last = lats - LANES
    base = count + sizes.words

    def fill(applied):
        def block(k, carry):
            start = pl.multiple_of(k * BITS, BITS)
            rows = pl.ds(start, BITS)
            ids = lane_ids(BITS)
            total = [jnp.zeros((BITS, LANES), F32) for _ in edges]
            for i in range(n + 2):
                if i >= n:
                    side = west_row if i == n else east_row
                    low, high = side[rows, 0:LANES], side[rows, last:]
                else:
                    if 0 < i < n - 1:
                        low, high = applied[i - 1, rows, 0:LANES], applied[i - 1, rows, last:]
                    else:
                        low, high = ends[min(i, 1), rows, 0:LANES], ends[min(i, 1), rows, last:]
                    low, high = low * ar[i : i + 1, 0:LANES], high * ar[i : i + 1, last:]
                moved = edge_rows_of(sizes, low, high, i)
                total = [jnp.where(ids == i, m, t) for m, t in zip(moved, total)]
            for edge, t in zip(edges, total):
                edge[rows, :] = t
            return carry

        lax.fori_loop(0, count // BITS, block, 0)

    pl.when(far_side())(lambda: fill(far))
    pl.when(jnp.logical_not(far_side()))(lambda: fill(near))
    tails = [jnp.zeros((8, LANES), F32) for _ in edges]
    ids, sub = lane_ids(8), lax.broadcasted_iota(jnp.int32, (8, LANES), 0)
    for k, row in enumerate((base, base + 2)):
        ends = [ref[row : row + 1, :] for ref in (west_row, east_row)]
        for side, end in enumerate(ends):
            moved = edge_rows_of(
                sizes,
                jnp.broadcast_to(end[:, 0:LANES], (8, LANES)),
                jnp.broadcast_to(end[:, last:], (8, LANES)),
                n + side,
            )
            spot = (ids == n + side) & (sub == k)
            tails = [jnp.where(spot, m, t) for m, t in zip(moved, tails)]
    for edge, t in zip(edges, tails):
        edge[count : count + 8, :] = t


def image_inner_kernel(part, sizes, near, far, coef_near, coef_far, ends, got_low, got_high, out):
    n, count = sizes.lons, sizes.count
    blocks = count // BITS // 2

    def fill(applied, coef):
        def block(k, carry):
            start = pl.multiple_of((part * blocks + k) * BITS, BITS)
            rows, here = pl.ds(start, BITS), pl.ds(pl.multiple_of(k * BITS, BITS), BITS)
            low_edge, high_edge = got_low[rows, :], got_high[rows, :]

            def get(i):
                source = applied[i - 1, rows, :] if 0 < i < n - 1 else ends[min(i, 1), rows, :]
                return [a * b for a, b in zip(halves(source), spread_row(coef, (5,), i))]

            west, middle = get(0), get(1)
            for i in range(1, n - 1):
                east = get(i + 1)
                north, south = lat_shifts(
                    middle, edge_at(low_edge, i, 0), edge_at(high_edge, i, LANES - 1)
                )
                weights = rows_of(coef, i)
                for h, tile in enumerate(stencil(weights, middle, east, west, north, south)):
                    out[i - 1, here, h * LANES : (h + 1) * LANES] = tile
                west, middle = middle, east
            return carry

        lax.fori_loop(0, blocks, block, 0)

    pl.when(far_side())(lambda: fill(far, coef_far))
    pl.when(jnp.logical_not(far_side()))(lambda: fill(near, coef_near))


def image_kernel(
    sizes, sk, ar, west_row, east_row, far_west, far_east, near, far, ends, end_coef,
    got_low, got_high, inner_0, inner_1, out, buffer, sems,
):
    n, count = sizes.lons, sizes.count
    base = count + sizes.words
    lat_id = lax.axis_index("lat")
    at_low = jnp.where(lat_id == 0, 0.0, 1.0)
    at_high = jnp.where(lat_id == sizes.lat_axis - 1, 0.0, 1.0)
    near_rows = [ref[base : base + 5, :] for ref in (west_row, east_row)]
    far_rows = [ref[count : count + 2, :] for ref in (far_west, far_east)]
    ghost = []
    for side in (0, 1):
        rows = near_rows[side]
        sea, east, north, kappa, area = (rows[k : k + 1] for k in range(5))
        if side == 0:
            east_w = get_row(end_coef, (2,), 0)
            west_w = far_rows[0][1:2] * far_rows[0][0:1] * sea
        else:
            east_w = east * sea * far_rows[1][0:1]
            west_w = get_row(end_coef, (1,), 1)
        lane = n + side
        low = got_low[count : count + 8, :]
        high = got_high[count : count + 8, :]
        edge_high = edge_at(high[0:1], lane, LANES - 1) * at_high
        edge_low = edge_at(low[0:1] * low[1:2], lane, 0) * at_low
        sea_parts = halves(sea)
        flow = halves(north * sea)
        sea_north, _ = lat_shifts(sea_parts, edge_low, edge_high)
        _, flow_south = lat_shifts(flow, edge_low, edge_high)
        north_w = jnp.concatenate([a * b for a, b in zip(flow, sea_north)], axis=1)
        south_w = jnp.concatenate([a * b for a, b in zip(flow_south, sea_parts)], axis=1)
        center = sea * (kappa + east_w + west_w + north_w + south_w)
        ghost.append(list(zip(*[halves(r * area) for r in (center, east_w, west_w, north_w, south_w)])))

    far_lon = far_side()
    copies = []
    for part, inner in enumerate((inner_0, inner_1)):
        columns = pl.ds(part * (count // 2), count // 2)
        copies += [(inner.at[i - 1], out.at[columns, i, :]) for i in range(1, n - 1)]
    copies += [(buffer.at[side], out.at[:, i, :]) for side, i in enumerate((0, n - 1))]
    copies = [pltpu.make_async_copy(a, b, sems.at[k]) for k, (a, b) in enumerate(copies)]
    for copy in copies[:-2]:
        copy.start()

    def block(k, carry):
        start = pl.multiple_of(k * BITS, BITS)
        rows = pl.ds(start, BITS)
        low_edge, high_edge = got_low[rows, :], got_high[rows, :]
        for side, i in enumerate((0, n - 1)):
            middle = halves((west_row, east_row)[side][rows, :])
            beyond = halves((far_west, far_east)[side][rows, :])
            own = halves(sk[i, rows, :])
            east, west = (own, beyond) if side == 0 else (beyond, own)
            north, south = lat_shifts(
                middle,
                edge_at(low_edge, n + side, 0),
                edge_at(high_edge, n + side, LANES - 1),
            )
            outer = stencil(ghost[side], middle, east, west, north, south)
            middle = halves(ends[side, rows, :] * ar[i : i + 1, :])
            next_in = 1 if side == 0 else n - 2
            inward = lax.select(far_lon, far[next_in - 1, rows, :], near[next_in - 1, rows, :])
            inward = halves(inward * ar[next_in : next_in + 1, :])
            east, west = (inward, outer) if side == 0 else (outer, inward)
            north, south = lat_shifts(
                middle, edge_at(low_edge, i, 0), edge_at(high_edge, i, LANES - 1)
            )
            weights = rows_of(end_coef, side)
            for h, tile in enumerate(stencil(weights, middle, east, west, north, south)):
                buffer[side, rows, h * LANES : (h + 1) * LANES] = tile
        return carry

    lax.fori_loop(0, count // BITS, block, 0)
    for copy in copies[-2:]:
        copy.start()
    for copy in copies:
        copy.wait()


def call(kernel, sizes, outs, args, scratch=(), inputs=None, out_space=pltpu.VMEM, alias=None):
    outs = [o if isinstance(o, jax.ShapeDtypeStruct) else jax.ShapeDtypeStruct(o, F32) for o in outs]
    spaces = inputs or [pltpu.VMEM] * len(args)
    return pl.pallas_call(
        functools.partial(kernel, sizes),
        out_shape=outs,
        in_specs=[pl.BlockSpec(memory_space=space) for space in spaces],
        out_specs=[pl.BlockSpec(memory_space=out_space)] * len(outs),
        scratch_shapes=list(scratch),
        input_output_aliases=alias or {},
        compiler_params=pltpu.CompilerParams(vmem_limit_bytes=16 << 20),
    )(*args)


def exchanges():
    lons, lats = lax.axis_size("lon"), lax.axis_size("lat")
    steps = [[(i * lats + j, i * lats + (j ^ bit)) for i in range(lons) for j in range(lats)] for bit in powers(lats)]
    lon_bits = powers(lons)
    lon_bits[:2] = reversed(lon_bits[:2])
    steps += [
        [(i * lats + j, (i ^ bit) * lats + (lats - 1 - j)) for i in range(lons) for j in range(lats)]
        for bit in lon_bits
    ]
    return steps


def powers(limit):
    return [1 << k for k in range(limit.bit_length() - 1)]


def swap_edges(edges):
    count = lax.axis_size("lat")
    if len(edges) == 1:
        got = lax.ppermute(edges[0], "lat", [(0, 1), (1, 0)])
        return got, got
    low, high = edges
    from_low = lax.ppermute(high, "lat", [(i, (i + 1) % count) for i in range(count)])
    from_high = lax.ppermute(low, "lat", [((i + 1) % count, i) for i in range(count)])
    return from_low, from_high


def local(sketch, probe_bits, ocean, east_cond, north_cond, kappa_sq, inv_area):
    sizes = Sizes(sketch, probe_bits)
    n, lats, count = sizes.lons, sizes.lats, sizes.count
    lon_axis = lax.axis_size("lon")
    eastward = [(i, (i + 1) % lon_axis) for i in range(lon_axis)]
    westward = [((i + 1) % lon_axis, i) for i in range(lon_axis)]
    fields = (sketch, probe_bits, ocean, east_cond, north_cond, kappa_sq, inv_area)
    line, far_line = (sizes.rows, lats), (sizes.edge_rows, lats)
    edge = (sizes.edge_rows, LANES)
    edge_count = 1 if sizes.paired else 2

    shapes = [jax.ShapeDtypeStruct(f.shape, f.dtype) for f in fields]
    shapes[0] = jax.ShapeDtypeStruct((n, count, lats), F32)
    loaded = call(
        load_kernel,
        sizes,
        shapes + [line, line, far_line, far_line] + [(n + 1, max(count, (sizes.words + 2) * n), LANES)] * edge_count,
        [pltpu.with_memory_space_constraint(f, pltpu.HBM) for f in fields],
        [pltpu.SemaphoreType.DMA((6 + n,))],
        inputs=[pltpu.HBM] * len(fields),
    )
    fields, (to_east, to_west, far_to_east, far_to_west), packed = tuple(loaded[:7]), loaded[7:11], loaded[11:]
    sketch, probe_bits, ocean, east_cond, north_cond, kappa_sq, inv_area = fields
    west_row = lax.ppermute(to_east, "lon", eastward)
    east_row = lax.ppermute(to_west, "lon", westward)
    far_east = lax.ppermute(far_to_west, "lon", westward)
    low, high = swap_edges(packed)
    far_east = lax.ppermute(far_to_west, "lon", westward)
    far_west = lax.ppermute(far_to_east, "lon", eastward)

    def split(lons):
        return [pltpu.VMEM((sizes.cols, lons * lats), jnp.bfloat16)] * 2

    inner = [
        call(
            functools.partial(inner_kernel, far),
            sizes,
            [(n - 2, count, lats), (6, lats // LANES, n + 8, LANES), (sizes.cols, sizes.cols)],
            fields + (low, high),
            split(n - 2) + [pltpu.VMEM((2, n + 16, lats), F32), pltpu.VMEM((lats // LANES, n + 8, LANES), F32)],
        )
        for far in (False, True)
    ]
    (near, coef_near, partial_near), (far, coef_far, partial_far) = inner
    gram, ends, end_coef = call(
        gram_kernel,
        sizes,
        [(8 * len(FOLDS), LANES) if sizes.folded else (sizes.cols, sizes.cols), (2, count, lats), (5, lats // LANES, 16, LANES)],
        (sketch, probe_bits, ocean, east_cond, kappa_sq, inv_area, west_row, east_row, low, high)
        + (coef_near, coef_far, partial_near, partial_far),
        split(2) + [pltpu.VMEM((sizes.cols, LANES), F32)],
    )
    edges = call(edge_kernel, sizes, [edge] * edge_count, (inv_area, west_row, east_row, near, far, ends))
    low2, high2 = swap_edges(edges)
    inner_images = [
        call(
            functools.partial(image_inner_kernel, part),
            sizes,
            [(n - 2, count // 2, lats)],
            (near, far, coef_near, coef_far, ends, low2, high2),
        )[0]
        for part in range(2)
    ]
    (image,) = call(
        image_kernel,
        sizes,
        [(count, n, lats)],
        (sketch, inv_area, west_row, east_row, far_west, far_east, near, far, ends, end_coef, low2, high2)
        + tuple(inner_images),
        [pltpu.VMEM((2, count, lats), F32), pltpu.SemaphoreType.DMA((2 * n - 2,))],
        out_space=pltpu.HBM,
    )
    steps = exchanges()
    for k, pairs in enumerate(steps):
        other = lax.ppermute(gram, ("lon", "lat"), pairs)
        if k < len(steps) - 1:
            gram = gram + other
    (gram,) = call(unfold_kernel, sizes, [(sizes.cols, sizes.cols)], (gram, other))
    return image, gram


def solution(mesh):
    field, flat = P(None, "lon", "lat"), P("lon", "lat")
    return jax.shard_map(
        local,
        mesh=mesh,
        in_specs=(field, field, flat, flat, flat, flat, flat),
        out_specs=(field, P()),
        check_vma=False,
    )
```

```python
import functools

import jax
import jax.numpy as jnp
from jax import lax
from jax.experimental import pallas as pl
from jax.experimental.pallas import tpu as pltpu
from jax.sharding import PartitionSpec as P


LANES = 128
BITS = 16
FOLDS = ((8,), (7,), (6,), (5,), (9, 10, 11))
F32 = jnp.float32


def lane_ids(rows):
    return lax.broadcasted_iota(jnp.int32, (rows, LANES), 1)


def spread(words):
    shape = (BITS, words.shape[-1])
    shifts = lax.broadcasted_iota(jnp.int32, shape, 0)
    bits = jnp.bitwise_and(jnp.right_shift(jnp.broadcast_to(words, shape), shifts), 1)
    return (1 - 2 * bits).astype(F32)


def halves(field):
    return [field[:, h : h + LANES] for h in range(0, field.shape[-1], LANES)]


def lat_shifts(field, low_edge, high_edge):
    ids = lane_ids(field[0].shape[0])
    up = [pltpu.roll(part, LANES - 1, 1) for part in field] + [high_edge]
    down = [low_edge] + [pltpu.roll(part, 1, 1) for part in field]
    north = [jnp.where(ids == LANES - 1, up[h + 1], up[h]) for h in range(len(field))]
    south = [jnp.where(ids == 0, down[h], down[h + 1]) for h in range(len(field))]
    return north, south


def stencil(weights, middle, east, west, north, south):
    return [
        c * m - e * xe - w * xw - n * xn - s * xs
        for (c, e, w, n, s), m, xe, xw, xn, xs in zip(weights, middle, east, west, north, south)
    ]


def edge_at(edge, lane, target):
    return pltpu.roll(edge, (target - lane) % LANES, 1)


def fold_place(sizes, r, other):
    start = sizes.cols
    for before in FOLDS[r]:
        width = sizes.cols - 8 * before
        if before == other:
            return start % LANES, width
        start += width


class Sizes:
    def __init__(self, sketch, probe_bits):
        self.count, self.lons, self.lats = sketch.shape
        self.words = probe_bits.shape[0]
        self.cols = self.count + BITS * self.words
        self.rows = -(-(self.count + self.words + 5) // 8) * 8
        self.edge_rows = -(-(self.count + 2) // 8) * 8
        self.lat_axis = lax.axis_size("lat")
        self.paired = self.lat_axis == 2
        self.folded = 4 * self.cols == 3 * LANES
        self.cells = lax.axis_size("lon") * self.lons * self.lat_axis * self.lats


def edge_rows_of(sizes, low, high, lane):
    if sizes.paired:
        first = lax.axis_index("lat") == 0
        picked = lax.select(first, high, low)
        shift = jnp.where(first, (lane + 1) % LANES, lane)
        return [pltpu.roll(picked, shift, 1)]
    return [pltpu.roll(low, lane, 1), pltpu.roll(high, (lane + 1) % LANES, 1)]


def end_row(sizes, sk, wd, oc, fields, first, r):
    count, base = sizes.count, sizes.count + sizes.words
    first[0:count, :] = sk[r]
    for w in range(sizes.words):
        first[count + w : count + w + 1, :] = wd[w, r : r + 1, :].astype(F32)
    first[base : base + 1, :] = oc[r : r + 1, :].astype(F32)
    for k, ref in enumerate(fields):
        first[base + 1 + k : base + 2 + k, :] = ref[r : r + 1, :]
    rest = first.shape[0] - base - 5
    if rest:
        first[base + 5 :, :] = jnp.zeros((rest, sizes.lats), F32)


def load_kernel(sizes, *refs):
    given, held, rows, tiles, sems = refs[:7], refs[7:14], refs[14:18], refs[18:-1], refs[-1]
    n, count = sizes.lons, sizes.count
    last = sizes.lats - LANES
    low_first = lax.axis_index("lat") == 0
    pairs = [(given[0].at[:, i, :], held[0].at[i]) for i in range(n)]
    pairs += list(zip(given[1:], held[1:]))
    copies = [pltpu.make_async_copy(g, h, sems.at[k]) for k, (g, h) in enumerate(pairs)]
    for copy in copies:
        copy.start()
    sk, wd, oc, ea, no = held[:5]
    base = sizes.words * n

    def end(ref, k):
        low, high = ref[..., 0:LANES], ref[..., last:]
        if sizes.paired:
            return lax.select(low_first, high, low)
        return (low, high)[k]

    for copy in copies[n:]:
        copy.wait()
    for k, tile in enumerate(tiles):
        words = end(wd, k).astype(F32)
        for w in range(sizes.words):
            tile[n, w * n : (w + 1) * n, :] = words[w]
        tile[n, base : base + n, :] = end(oc, k).astype(F32)
        tile[n, base + n : base + 2 * n, :] = end(no, k)
    for i in range(n):
        copies[i].wait()
        for k, tile in enumerate(tiles):
            tile[i, 0:count] = end(sk.at[i], k)
        if i in (0, n - 1):
            end_row(sizes, sk, wd, oc, held[3:], rows[0 if i else 1], i)
        if i in (1, n - 2):
            ref = rows[3 if i == 1 else 2]
            ref[0:count, :] = sk[i]
            ref[count : count + 1, :] = oc[i : i + 1, :].astype(F32)
            ref[count + 1 : count + 2, :] = ea[i : i + 1, :]
            ref[count + 2 :, :] = jnp.zeros((ref.shape[0] - count - 2, sizes.lats), F32)


def far_side():
    return lax.axis_index("lon") >= 5


def products(split_hi, split_lo):
    dims = (((1,), (1,)), ((), ()))
    main = lax.dot_general(split_hi[...], split_hi[...], dims, preferred_element_type=F32)
    cross = lax.dot_general(split_hi[...], split_lo[...], dims, preferred_element_type=F32)
    return main + cross + cross.T


def store_split(split_hi, split_lo, rows, at, scaled):
    high = scaled.astype(jnp.bfloat16)
    split_hi[rows, at] = high
    split_lo[rows, at] = (scaled - high.astype(F32)).astype(jnp.bfloat16)


def put_row(ref, where, rows, field):
    for h, part in enumerate(halves(field)):
        ref[where + (h, rows)] = part


def get_row(ref, where, i):
    tiles = [ref[where + (h, slice(i, i + 1))] for h in range(ref.shape[-3])]
    return jnp.concatenate(tiles, axis=1)


def spread_row(ref, where, i):
    tiles = [ref[where + (h, pl.ds(i, 8, stride=0))] for h in range(ref.shape[-3])]
    return [jnp.concatenate([tile] * (BITS // 8), axis=0) for tile in tiles]


def rows_of(ref, i):
    return list(zip(*[spread_row(ref, (k,), i) for k in range(5)]))


def sketch_edges(got_low, got_high, rows):
    return lambda i: (pltpu.roll(got_low[i, rows, :], 1, 1), pltpu.roll(got_high[i, rows, :], LANES - 1, 1))


def probe_edges(sizes, w, got_low, got_high):
    n = sizes.lons

    def edges(i):
        at = w * n + i
        low, high = (got[n, at : at + 1, :].astype(jnp.int32) for got in (got_low, got_high))
        return spread(pltpu.roll(low, 1, 1)), spread(pltpu.roll(high, LANES - 1, 1))

    return edges


def inner_kernel(
    far, sizes, sk, wd, oc, ea, no, ka, ar, got_low, got_high,
    applied, coef, partial, split_hi, split_lo, ext, root,
):
    n, count, lats, words = sizes.lons, sizes.count, sizes.lats, sizes.words

    @pl.when(far_side() == far)
    def _():
        lat_id = lax.axis_index("lat")
        sea = oc[...].astype(F32)
        ext[0, 8 : 8 + n, :] = sea
        ext[0, 8 + n : 9 + n, :] = jnp.zeros((1, lats), F32)
        ext[1, 8 : 8 + n, :] = ea[...] * sea * ext[0, 9 : 9 + n, :]
        ext[1, 7:8, :] = jnp.zeros((1, lats), F32)
        east_w = ext[1, 8 : 8 + n, :]
        west_w = ext[1, 7 : 7 + n, :]

        sea_parts = halves(sea)
        half_north = [no[:, h * LANES : (h + 1) * LANES] * part for h, part in enumerate(sea_parts)]
        at_low = jnp.where(lat_id == 0, 0.0, 1.0)
        at_high = jnp.where(lat_id == sizes.lat_axis - 1, 0.0, 1.0)
        edge_high = pltpu.roll(got_high[n, words * n : (words + 1) * n, :], LANES - 1, 1) * at_high
        flow_low = got_low[n, words * n : (words + 1) * n, :] * got_low[n, (words + 1) * n : (words + 2) * n, :]
        edge_low = pltpu.roll(flow_low, 1, 1) * at_low
        sea_north, _ = lat_shifts(sea_parts, edge_low, edge_high)
        _, flow_south = lat_shifts(half_north, edge_low, edge_high)
        north_w = jnp.concatenate([a * b for a, b in zip(half_north, sea_north)], axis=1)
        south_w = jnp.concatenate([a * b for a, b in zip(flow_south, sea_parts)], axis=1)
        rooted = jnp.sqrt(ar[...])
        center = sea * (ka[...] + east_w + west_w + north_w + south_w)
        for k, field in enumerate((center, east_w, west_w, north_w, south_w)):
            put_row(coef, (k,), slice(0, n), field)
            put_row(root, (k,), slice(0, n), field * rooted)
        put_row(coef, (5,), slice(0, n), rooted)

        def one_block(start, get, edges, keep):
            rows = pl.ds(start, BITS)
            west, middle = get(0), get(1)
            for i in range(1, n - 1):
                east = get(i + 1)
                north, south = lat_shifts(middle, *edges(i))
                weights = rows_of(root, i)
                for h, part in enumerate(stencil(weights, middle, east, west, north, south)):
                    here = slice(h * LANES, (h + 1) * LANES)
                    if keep:
                        applied[i - 1, rows, here] = part
                    at = slice((i - 1) * lats + h * LANES, (i - 1) * lats + (h + 1) * LANES)
                    store_split(split_hi, split_lo, rows, at, part)
                west, middle = middle, east

        def sketch_block(k, carry):
            start = pl.multiple_of(k * BITS, BITS)
            rows = pl.ds(start, BITS)
            one_block(start, lambda i: halves(sk[i, rows, :]), sketch_edges(got_low, got_high, rows), True)
            return carry

        lax.fori_loop(0, count // BITS, sketch_block, 0)
        for w in range(words):
            one_block(
                count + w * BITS,
                lambda i: [spread(part) for part in halves(wd[w, i : i + 1, :])],
                probe_edges(sizes, w, got_low, got_high),
                False,
            )
        partial[...] = products(split_hi, split_lo)


def gram_kernel(
    sizes, sk, wd, oc, ea, ka, ar, west_row, east_row, got_low, got_high,
    coef_near, coef_far, partial_near, partial_far,
    gram, ends, end_coef, split_hi, split_lo, whole,
):
    n, count, lats, words = sizes.lons, sizes.count, sizes.lats, sizes.words
    base = count + words
    far = far_side()

    def inner(k, i):
        return lax.select(far, get_row(coef_far, (k,), i), get_row(coef_near, (k,), i))

    for side, i in enumerate((0, n - 1)):
        sea = oc[i : i + 1, :].astype(F32)
        east_w, west_w, north_w, south_w = (inner(k, i) for k in range(1, 5))
        if side == 0:
            west_w = west_row[base + 1 : base + 2, :] * west_row[base : base + 1, :] * sea
        else:
            east_w = ea[i : i + 1, :] * sea * east_row[base : base + 1, :]
        center = sea * (ka[i : i + 1, :] + east_w + west_w + north_w + south_w)
        for k, row in enumerate((center, east_w, west_w, north_w, south_w)):
            put_row(end_coef, (k,), slice(side, side + 1), row)
            put_row(end_coef, (k,), slice(8 + side, 9 + side), row * jnp.sqrt(ar[i : i + 1, :]))

    def one_block(start, get, edges, keep):
        rows = pl.ds(start, BITS)
        for side, i in enumerate((0, n - 1)):
            middle = get(i)
            north, south = lat_shifts(middle, *edges(i))
            weights = rows_of(end_coef, 8 + side)
            for h, part in enumerate(stencil(weights, middle, get(i + 1), get(i - 1), north, south)):
                here = slice(h * LANES, (h + 1) * LANES)
                if keep:
                    ends[side, rows, here] = part
                at = slice(side * lats + h * LANES, side * lats + (h + 1) * LANES)
                store_split(split_hi, split_lo, rows, at, part)

    for start in range(0, count, BITS):
        rows = slice(start, start + BITS)

        def get(i):
            if i == -1:
                return halves(west_row[rows, :])
            if i == n:
                return halves(east_row[rows, :])
            return halves(sk[i, rows, :])

        one_block(start, get, sketch_edges(got_low, got_high, rows), True)
    for w in range(words):

        def get(i):
            if i == -1:
                row = west_row[count + w : count + w + 1, :].astype(jnp.int32)
            elif i == n:
                row = east_row[count + w : count + w + 1, :].astype(jnp.int32)
            else:
                row = wd[w, i : i + 1, :]
            return [spread(part) for part in halves(row)]

        one_block(count + w * BITS, get, probe_edges(sizes, w, got_low, got_high), False)

    total = lax.select(far, partial_far[...], partial_near[...]) + products(split_hi, split_lo)
    if not sizes.folded:
        gram[...] = total
        return
    whole[:, 0 : sizes.cols] = total
    ids = lane_ids(8)
    for r, parts in enumerate(FOLDS):
        kept = whole[8 * r : 8 * r + 8, :]
        for other in parts:
            start, width = fold_place(sizes, r, other)
            moved = pltpu.roll(whole[8 * other : 8 * other + 8, :], (start - 8 * other) % LANES, 1)
            kept = jnp.where((ids - start) % LANES < width, moved, kept)
        gram[8 * r : 8 * r + 8, :] = kept


def unfold_kernel(sizes, mine, other, out):
    total = (mine[...] + other[...]) / sizes.cells
    if not sizes.folded:
        out[...] = total
        return
    blocks = {}
    for r, parts in enumerate(FOLDS):
        kept = total[8 * r : 8 * r + 8, :]
        blocks[r] = kept
        for other in parts:
            start, _ = fold_place(sizes, r, other)
            blocks[other] = pltpu.roll(kept, (8 * other - start) % LANES, 1)
    rows = [blocks[r] for r in sorted(blocks)]
    upper = jnp.concatenate(rows + [jnp.zeros((LANES - sizes.cols, LANES), F32)], axis=0)
    across = lane_ids(LANES) // 8
    down = lax.broadcasted_iota(jnp.int32, (LANES, LANES), 0) // 8
    out[...] = jnp.where(down <= across, upper, upper.T)[0 : sizes.cols, 0 : sizes.cols]


def edge_kernel(sizes, ar, west_row, east_row, near, far, ends, *edges):
    n, count, lats = sizes.lons, sizes.count, sizes.lats
    last = lats - LANES
    rooted = jnp.sqrt(ar[...])
    base = count + sizes.words

    def fill(applied):
        def block(k, carry):
            start = pl.multiple_of(k * BITS, BITS)
            rows = pl.ds(start, BITS)
            ids = lane_ids(BITS)
            total = [jnp.zeros((BITS, LANES), F32) for _ in edges]
            for i in range(n + 2):
                if i >= n:
                    side = west_row if i == n else east_row
                    low, high = side[rows, 0:LANES], side[rows, last:]
                else:
                    if 0 < i < n - 1:
                        low, high = applied[i - 1, rows, 0:LANES], applied[i - 1, rows, last:]
                    else:
                        low, high = ends[min(i, 1), rows, 0:LANES], ends[min(i, 1), rows, last:]
                    low, high = low * rooted[i : i + 1, 0:LANES], high * rooted[i : i + 1, last:]
                moved = edge_rows_of(sizes, low, high, i)
                total = [jnp.where(ids == i, m, t) for m, t in zip(moved, total)]
            for edge, t in zip(edges, total):
                edge[rows, :] = t
            return carry

        lax.fori_loop(0, count // BITS, block, 0)

    pl.when(far_side())(lambda: fill(far))
    pl.when(jnp.logical_not(far_side()))(lambda: fill(near))
    tails = [jnp.zeros((8, LANES), F32) for _ in edges]
    ids, sub = lane_ids(8), lax.broadcasted_iota(jnp.int32, (8, LANES), 0)
    for k, row in enumerate((base, base + 2)):
        ends = [ref[row : row + 1, :] for ref in (west_row, east_row)]
        for side, end in enumerate(ends):
            moved = edge_rows_of(
                sizes,
                jnp.broadcast_to(end[:, 0:LANES], (8, LANES)),
                jnp.broadcast_to(end[:, last:], (8, LANES)),
                n + side,
            )
            spot = (ids == n + side) & (sub == k)
            tails = [jnp.where(spot, m, t) for m, t in zip(moved, tails)]
    for edge, t in zip(edges, tails):
        edge[count : count + 8, :] = t


def image_inner_kernel(part, sizes, near, far, coef_near, coef_far, ends, got_low, got_high, out):
    n, count = sizes.lons, sizes.count
    blocks = count // BITS // 2

    def fill(applied, coef):
        def block(k, carry):
            start = pl.multiple_of((part * blocks + k) * BITS, BITS)
            rows, here = pl.ds(start, BITS), pl.ds(pl.multiple_of(k * BITS, BITS), BITS)
            low_edge, high_edge = got_low[rows, :], got_high[rows, :]

            def get(i):
                source = applied[i - 1, rows, :] if 0 < i < n - 1 else ends[min(i, 1), rows, :]
                return [a * b for a, b in zip(halves(source), spread_row(coef, (5,), i))]

            west, middle = get(0), get(1)
            for i in range(1, n - 1):
                east = get(i + 1)
                north, south = lat_shifts(
                    middle, edge_at(low_edge, i, 0), edge_at(high_edge, i, LANES - 1)
                )
                weights = rows_of(coef, i)
                for h, tile in enumerate(stencil(weights, middle, east, west, north, south)):
                    out[i - 1, here, h * LANES : (h + 1) * LANES] = tile
                west, middle = middle, east
            return carry

        lax.fori_loop(0, blocks, block, 0)

    pl.when(far_side())(lambda: fill(far, coef_far))
    pl.when(jnp.logical_not(far_side()))(lambda: fill(near, coef_near))


def image_kernel(
    sizes, sk, ar, west_row, east_row, far_west, far_east, near, far, ends, end_coef,
    got_low, got_high, inner_0, inner_1, out, buffer, sems,
):
    n, count = sizes.lons, sizes.count
    base = count + sizes.words
    lat_id = lax.axis_index("lat")
    at_low = jnp.where(lat_id == 0, 0.0, 1.0)
    at_high = jnp.where(lat_id == sizes.lat_axis - 1, 0.0, 1.0)
    near_rows = [ref[base : base + 5, :] for ref in (west_row, east_row)]
    far_rows = [ref[count : count + 2, :] for ref in (far_west, far_east)]
    ghost = []
    for side in (0, 1):
        rows = near_rows[side]
        sea, east, north, kappa, area = (rows[k : k + 1] for k in range(5))
        if side == 0:
            east_w = get_row(end_coef, (2,), 0)
            west_w = far_rows[0][1:2] * far_rows[0][0:1] * sea
        else:
            east_w = east * sea * far_rows[1][0:1]
            west_w = get_row(end_coef, (1,), 1)
        lane = n + side
        low = got_low[count : count + 8, :]
        high = got_high[count : count + 8, :]
        edge_high = edge_at(high[0:1], lane, LANES - 1) * at_high
        edge_low = edge_at(low[0:1] * low[1:2], lane, 0) * at_low
        sea_parts = halves(sea)
        flow = halves(north * sea)
        sea_north, _ = lat_shifts(sea_parts, edge_low, edge_high)
        _, flow_south = lat_shifts(flow, edge_low, edge_high)
        north_w = jnp.concatenate([a * b for a, b in zip(flow, sea_north)], axis=1)
        south_w = jnp.concatenate([a * b for a, b in zip(flow_south, sea_parts)], axis=1)
        center = sea * (kappa + east_w + west_w + north_w + south_w)
        ghost.append(list(zip(*[halves(r * area) for r in (center, east_w, west_w, north_w, south_w)])))

    far_lon = far_side()
    copies = []
    for part, inner in enumerate((inner_0, inner_1)):
        columns = pl.ds(part * (count // 2), count // 2)
        copies += [(inner.at[i - 1], out.at[columns, i, :]) for i in range(1, n - 1)]
    copies += [(buffer.at[side], out.at[:, i, :]) for side, i in enumerate((0, n - 1))]
    copies = [pltpu.make_async_copy(a, b, sems.at[k]) for k, (a, b) in enumerate(copies)]
    for copy in copies[:-2]:
        copy.start()

    def block(k, carry):
        start = pl.multiple_of(k * BITS, BITS)
        rows = pl.ds(start, BITS)
        low_edge, high_edge = got_low[rows, :], got_high[rows, :]
        for side, i in enumerate((0, n - 1)):
            middle = halves((west_row, east_row)[side][rows, :])
            beyond = halves((far_west, far_east)[side][rows, :])
            own = halves(sk[i, rows, :])
            east, west = (own, beyond) if side == 0 else (beyond, own)
            north, south = lat_shifts(
                middle,
                edge_at(low_edge, n + side, 0),
                edge_at(high_edge, n + side, LANES - 1),
            )
            outer = stencil(ghost[side], middle, east, west, north, south)
            middle = halves(ends[side, rows, :] * jnp.sqrt(ar[i : i + 1, :]))
            next_in = 1 if side == 0 else n - 2
            inward = lax.select(far_lon, far[next_in - 1, rows, :], near[next_in - 1, rows, :])
            inward = halves(inward * jnp.sqrt(ar[next_in : next_in + 1, :]))
            east, west = (inward, outer) if side == 0 else (outer, inward)
            north, south = lat_shifts(
                middle, edge_at(low_edge, i, 0), edge_at(high_edge, i, LANES - 1)
            )
            weights = rows_of(end_coef, side)
            for h, tile in enumerate(stencil(weights, middle, east, west, north, south)):
                buffer[side, rows, h * LANES : (h + 1) * LANES] = tile
        return carry

    lax.fori_loop(0, count // BITS, block, 0)
    for copy in copies[-2:]:
        copy.start()
    for copy in copies:
        copy.wait()


def call(kernel, sizes, outs, args, scratch=(), inputs=None, out_space=pltpu.VMEM, alias=None):
    outs = [o if isinstance(o, jax.ShapeDtypeStruct) else jax.ShapeDtypeStruct(o, F32) for o in outs]
    spaces = inputs or [pltpu.VMEM] * len(args)
    return pl.pallas_call(
        functools.partial(kernel, sizes),
        out_shape=outs,
        in_specs=[pl.BlockSpec(memory_space=space) for space in spaces],
        out_specs=[pl.BlockSpec(memory_space=out_space)] * len(outs),
        scratch_shapes=list(scratch),
        input_output_aliases=alias or {},
        compiler_params=pltpu.CompilerParams(vmem_limit_bytes=16 << 20),
    )(*args)


def exchanges():
    lons, lats = lax.axis_size("lon"), lax.axis_size("lat")
    steps = [[(i * lats + j, i * lats + (j ^ bit)) for i in range(lons) for j in range(lats)] for bit in powers(lats)]
    lon_bits = powers(lons)
    lon_bits[:2] = reversed(lon_bits[:2])
    steps += [
        [(i * lats + j, (i ^ bit) * lats + (lats - 1 - j)) for i in range(lons) for j in range(lats)]
        for bit in lon_bits
    ]
    return steps


def powers(limit):
    return [1 << k for k in range(limit.bit_length() - 1)]


def swap_edges(edges):
    count = lax.axis_size("lat")
    if len(edges) == 1:
        got = lax.ppermute(edges[0], "lat", [(0, 1), (1, 0)])
        return got, got
    low, high = edges
    from_low = lax.ppermute(high, "lat", [(i, (i + 1) % count) for i in range(count)])
    from_high = lax.ppermute(low, "lat", [((i + 1) % count, i) for i in range(count)])
    return from_low, from_high


def local(sketch, probe_bits, ocean, east_cond, north_cond, kappa_sq, inv_area):
    sizes = Sizes(sketch, probe_bits)
    n, lats, count = sizes.lons, sizes.lats, sizes.count
    lon_axis = lax.axis_size("lon")
    eastward = [(i, (i + 1) % lon_axis) for i in range(lon_axis)]
    westward = [((i + 1) % lon_axis, i) for i in range(lon_axis)]
    fields = (sketch, probe_bits, ocean, east_cond, north_cond, kappa_sq, inv_area)
    line, far_line = (sizes.rows, lats), (sizes.edge_rows, lats)
    edge = (sizes.edge_rows, LANES)
    edge_count = 1 if sizes.paired else 2

    shapes = [jax.ShapeDtypeStruct(f.shape, f.dtype) for f in fields]
    shapes[0] = jax.ShapeDtypeStruct((n, count, lats), F32)
    loaded = call(
        load_kernel,
        sizes,
        shapes + [line, line, far_line, far_line] + [(n + 1, max(count, (sizes.words + 2) * n), LANES)] * edge_count,
        [pltpu.with_memory_space_constraint(f, pltpu.HBM) for f in fields],
        [pltpu.SemaphoreType.DMA((6 + n,))],
        inputs=[pltpu.HBM] * len(fields),
    )
    fields, (to_east, to_west, far_to_east, far_to_west), packed = tuple(loaded[:7]), loaded[7:11], loaded[11:]
    sketch, probe_bits, ocean, east_cond, north_cond, kappa_sq, inv_area = fields
    west_row = lax.ppermute(to_east, "lon", eastward)
    east_row = lax.ppermute(to_west, "lon", westward)
    far_east = lax.ppermute(far_to_west, "lon", westward)
    low, high = swap_edges(packed)
    far_east = lax.ppermute(far_to_west, "lon", westward)
    far_west = lax.ppermute(far_to_east, "lon", eastward)

    def split(lons):
        return [pltpu.VMEM((sizes.cols, lons * lats), jnp.bfloat16)] * 2

    inner = [
        call(
            functools.partial(inner_kernel, far),
            sizes,
            [(n - 2, count, lats), (6, lats // LANES, n + 8, LANES), (sizes.cols, sizes.cols)],
            fields + (low, high),
            split(n - 2) + [pltpu.VMEM((2, n + 16, lats), F32), pltpu.VMEM((5, lats // LANES, n + 8, LANES), F32)],
        )
        for far in (False, True)
    ]
    (near, coef_near, partial_near), (far, coef_far, partial_far) = inner
    gram, ends, end_coef = call(
        gram_kernel,
        sizes,
        [(8 * len(FOLDS), LANES) if sizes.folded else (sizes.cols, sizes.cols), (2, count, lats), (5, lats // LANES, 24, LANES)],
        (sketch, probe_bits, ocean, east_cond, kappa_sq, inv_area, west_row, east_row, low, high)
        + (coef_near, coef_far, partial_near, partial_far),
        split(2) + [pltpu.VMEM((sizes.cols, LANES), F32)],
    )
    edges = call(edge_kernel, sizes, [edge] * edge_count, (inv_area, west_row, east_row, near, far, ends))
    low2, high2 = swap_edges(edges)
    inner_images = [
        call(
            functools.partial(image_inner_kernel, part),
            sizes,
            [(n - 2, count // 2, lats)],
            (near, far, coef_near, coef_far, ends, low2, high2),
        )[0]
        for part in range(2)
    ]
    (image,) = call(
        image_kernel,
        sizes,
        [(count, n, lats)],
        (sketch, inv_area, west_row, east_row, far_west, far_east, near, far, ends, end_coef, low2, high2)
        + tuple(inner_images),
        [pltpu.VMEM((2, count, lats), F32), pltpu.SemaphoreType.DMA((2 * n - 2,))],
        out_space=pltpu.HBM,
    )
    steps = exchanges()
    for k, pairs in enumerate(steps):
        other = lax.ppermute(gram, ("lon", "lat"), pairs)
        if k < len(steps) - 1:
            gram = gram + other
    (gram,) = call(unfold_kernel, sizes, [(sizes.cols, sizes.cols)], (gram, other))
    return image, gram


def solution(mesh):
    field, flat = P(None, "lon", "lat"), P("lon", "lat")
    return jax.shard_map(
        local,
        mesh=mesh,
        in_specs=(field, field, flat, flat, flat, flat, flat),
        out_specs=(field, P()),
        check_vma=False,
    )
```
